256 devices in a mesh: req: 64 (over z, x, core), tp: 4 (over y).
Axes of the slice: x: 4, y: 4, z: 8, core: 2. Of those that a mesh axis runs over, the one named last changes fastest.
Arguments:
- hidden_in: bfloat16 [32768, 1024], P('req', 'tp'), may hold values from -6 to 6
- w_qkv: bfloat16 [1024, 3, 1024], P(None, None, 'tp'), may hold values from -0.1875 to 0.1875
- w_out: bfloat16 [1024, 1024], P('tp'), may hold values from -0.75 to 0.75
- first_gain: float32 [1024], replicated, may hold values from 0.1 to 1.9
- w_up: bfloat16 [1024, 4096], P(None, 'tp'), may hold values from -0.1875 to 0.1875
- w_down: bfloat16 [4096, 1024], P('tp'), may hold values from -0.09375 to 0.09375
- second_gain: float32 [1024], replicated, may hold values from 0.1 to 1.9
- cache_pool: bfloat16 [4096, 128, 2, 1024], P('req', None, None, 'tp'), may hold values from -600 to 600
- page_table: int32 [512, 8], P('req'), may hold values from 0 to 63, as said below
- cache_len: int32 [512], P('req'), may hold values from 1 to 1024, as said below
- tree_parent: int32 [512, 64], P('req'), may hold values from -1 to 62, as said below
- accept_node: int32 [512], P('req'), may hold values from 0 to 63
Outputs:
- layer_out: bfloat16 [32768, 1024], P('req', 'tp')
- accepted_kv: bfloat16 [512, 64, 2, 1024], P('req', None, None, 'tp')
The draws below stay inside these ranges and needn't reach their ends.
Inputs may be any that keep to these rules, and one draw needn't show every extreme that they name: `page_table`: on each index e of req, the 8 x 8 entries of its rows are a permutation of the slots 0 to 63; row j, column m holds the slot in e's pool of page j of member m of the index e - j of req (modulo the axis size). `cache_len`: on each index of req exactly 2 requests have lengths over 256, and the others at most 256; the length 1024 occurs in every draw, and so does the length 256. `tree_parent`: node 0 is the root with parent -1; every other node's parent is an earlier node.
All inputs are finite; a program needn't handle non-finite values.
Results may differ from the reference program's by a relative error of at most 0.012.
Values may be sent and summed in bfloat16 or wider, within the bound.
A program may use at most 128 MiB of HBM per device.

```python
import jax
import jax.numpy as jnp
from jax import lax

D = 1024
H = 16
HD = 64
FF = 4096
DRAFT = 64
PAGE = 128
MAXPG = 8
REQ_DEV = 8
LONG_DEV = 2
REQS = 512
TOKENS = 32768
POOL_DEV = 64
POOL = 4096
PAGE_ROWS = 512
N_REQ = 64


def draw_cache_pool(key, part):
    shape = (POOL, PAGE, 2, H * HD)
    keys = jax.random.split(key, 1)
    base = jnp.clip(jax.random.normal(keys[0], shape, jnp.float32), -6.0, 6.0)
    return base.astype(jnp.bfloat16)


def draw_page_table(key, part):
    groups = PAGE_ROWS // MAXPG
    keys = jax.random.split(key, groups)
    perms = jax.vmap(lambda one_key: jax.random.permutation(one_key, POOL_DEV))(keys)
    return perms.reshape(PAGE_ROWS, REQ_DEV).astype(jnp.int32)


def draw_cache_len(key, part):
    keys = jax.random.split(key, 5)
    groups = REQS // REQ_DEV
    longest = MAXPG * PAGE
    group_keys = jax.random.split(keys[0], groups)
    ranks = jax.vmap(lambda one_key: jax.random.permutation(one_key, REQ_DEV))(group_keys)
    group_ids = jnp.broadcast_to(jnp.arange(groups, dtype=jnp.int32)[:, None], (groups, REQ_DEV))
    is_long = ranks < LONG_DEV
    short_len = jax.random.randint(keys[1], (groups, REQ_DEV), 1, 2 * PAGE + 1)
    long_len = jax.random.randint(keys[2], (groups, REQ_DEV), longest // 2 + 1, longest + 1)
    lengths = jnp.where(is_long, long_len, short_len)
    forced_long = jax.random.randint(keys[3], (), 0, groups)
    forced_short = jax.random.randint(keys[4], (), 0, groups)
    lengths = jnp.where((group_ids == forced_long) & (ranks == 0), longest, lengths)
    lengths = jnp.where((group_ids == forced_short) & (ranks == REQ_DEV - 1) & (ranks >= LONG_DEV), 2 * PAGE, lengths)
    return lengths.reshape(REQS).astype(jnp.int32)


def draw_tree_parent(key, part):
    index = jnp.arange(DRAFT, dtype=jnp.int32)[None, :]
    back = jax.random.randint(key, (REQS, DRAFT), 0, 3)
    parent = jnp.maximum(index - 1 - back, 0)
    parent = jnp.where(index == 0, -1, parent)
    return parent.astype(jnp.int32)


def plant(array, key, smallest, high):
    shape = array.shape
    index_at = [jax.random.randint(jax.random.fold_in(key, axis), (), 0, shape[axis]) for axis in range(len(shape))]
    array = array.at[tuple(index_at)].set(smallest)
    longest = shape.index(max(shape))
    index_at[longest] = (index_at[longest] + 1) % shape[longest]
    return array.at[tuple(index_at)].set(high)


def block_scale(own_key, dims, cuts, low, largest):
    def one(axis_at, blocks):
        heights = jax.random.uniform(jax.random.fold_in(jax.random.fold_in(own_key, 6), axis_at), (blocks,), jnp.float32, low / len(cuts), largest / len(cuts))
        return jnp.repeat(jnp.exp(heights), dims[axis_at] // blocks).reshape((-1,) + (1,) * (len(dims) - axis_at - 1))

    level = one(*cuts[0])
    for cut in cuts[1:]:
        level = level * one(*cut)
    return level


def normal_values(key, extent, deviation, most, cuts=(), kind=jnp.bfloat16):
    array = jax.random.normal(key, extent, jnp.float32) * deviation
    if len(cuts) > 0:
        array = block_scale(key, extent, cuts, -0.22, 0.18) * array
    return jnp.clip(array, min=-most, max=most).astype(kind)


def setup_inputs(seed: int = 0) -> dict:
    splits = jax.random.split(jax.random.key(seed), 13)
    return {
        "hidden_in": normal_values(splits[0], (TOKENS, D), 1.0, 6.0, ((0, 64), (1, 4))),
        "w_qkv": normal_values(splits[1], (D, 3, H * HD), D ** -0.5, 0.1875, ((2, 4),)),
        "w_out": normal_values(splits[2], (H * HD, D), (H * HD // 16) ** -0.5, 0.75, ((0, 4),)),
        "first_gain": jnp.clip(1.0 + 0.18 * jax.random.normal(splits[3], (D,), jnp.float32), 0.1, 1.9),
        "w_up": normal_values(splits[4], (D, FF), D ** -0.5, 0.1875, ((1, 4),)),
        "w_down": normal_values(splits[5], (FF, D), FF ** -0.5, 0.09375, ((0, 4),)),
        "second_gain": jnp.clip(1.0 + 0.18 * jax.random.normal(splits[6], (D,), jnp.float32), 0.1, 1.9),
        "cache_pool": draw_cache_pool(jax.random.fold_in(splits[12], 71), 0),
        "page_table": draw_page_table(jax.random.fold_in(splits[12], 71), 0),
        "cache_len": draw_cache_len(jax.random.fold_in(splits[12], 71), 0),
        "tree_parent": draw_tree_parent(jax.random.fold_in(splits[12], 71), 0),
        "accept_node": plant(jax.random.randint(splits[11], (REQS,), 0, DRAFT), jax.random.fold_in(splits[11], 1), 0, DRAFT - 1).astype(jnp.int32),
    }


NEG = -1e+30
EPS = 1e-05

def block_partial(queries, key_rows, value_rows, valid):
    scores = jnp.einsum('bqhd,bkhd->bhqk', queries.astype(jnp.float32), key_rows.astype(jnp.float32), precision=lax.Precision.HIGHEST)
    allowed = valid[:, None, :, :]
    maxima = lax.optimization_barrier(jnp.max(jnp.where(allowed, scores, NEG), axis=-1))
    weights = jnp.where(allowed, jnp.exp(scores - maxima[..., None]), 0.0).astype(jnp.bfloat16)
    totals = lax.optimization_barrier(jnp.sum(weights.astype(jnp.float32), axis=-1))
    mixture = jnp.einsum('bhqk,bkhd->bqhd', weights.astype(jnp.float32), value_rows.astype(jnp.float32), precision=lax.Precision.HIGHEST)
    return (mixture, maxima, totals)

def combine_blocks(mixture, maxima, totals):
    best = lax.optimization_barrier(jnp.max(maxima, axis=0))
    scale = jnp.swapaxes(jnp.exp(maxima - best[None]), -1, -2)
    numer = lax.optimization_barrier(jnp.sum(mixture * scale[..., None], axis=0))
    denom = lax.optimization_barrier(jnp.sum(jnp.swapaxes(totals, -1, -2) * scale, axis=0))
    return numer / denom[..., None]

def ancestors(parents):
    count = parents.shape[-1]
    reach = jax.nn.one_hot(parents, count, dtype=jnp.float32) + jnp.eye(count, dtype=jnp.float32)
    for sweep in range(max(1, (count - 1).bit_length())):
        reach = jnp.minimum(jnp.einsum('rij,rjk->rik', reach, reach, precision=lax.Precision.HIGHEST), 1.0)
    return reach

def layer_norm(values, gain):
    width_all = values.shape[-1]
    center = lax.optimization_barrier(jnp.sum(values, axis=-1, keepdims=True)) / width_all
    spread = lax.optimization_barrier(jnp.sum(values * values, axis=-1, keepdims=True)) / width_all - center * center
    return (values - center) * lax.rsqrt(spread + EPS) * gain

def reference(hidden_in, w_qkv, w_out, first_gain, w_up, w_down, second_gain, cache_pool, page_table, cache_len, tree_parent, accept_node):
    width_all = H * HD
    projected = jnp.dot(hidden_in, w_qkv.reshape(D, 3 * width_all), preferred_element_type=jnp.float32)
    queries = (projected[:, :width_all] * 0.125).astype(jnp.bfloat16).reshape(REQS, DRAFT, H, HD)
    key_new = projected[:, width_all:2 * width_all].astype(jnp.bfloat16).reshape(REQS, DRAFT, H, HD)
    value_new = projected[:, 2 * width_all:].astype(jnp.bfloat16).reshape(REQS, DRAFT, H, HD)
    reach = ancestors(tree_parent)
    offsets = jnp.arange(MAXPG, dtype=jnp.int32)
    positions = offsets[:, None] * PAGE + jnp.arange(PAGE, dtype=jnp.int32)[None, :]

    def one_request(request):
        owner = request // REQ_DEV
        member = request % REQ_DEV
        device_ids = (owner + offsets) % N_REQ
        slot_ids = page_table[device_ids * MAXPG + offsets, member]
        page_rows = cache_pool[device_ids * POOL_DEV + slot_ids]
        key_rows = page_rows[:, :, 0].reshape(MAXPG, PAGE, H, HD)
        value_rows = page_rows[:, :, 1].reshape(MAXPG, PAGE, H, HD)
        own_queries = queries[request]
        valid = jnp.broadcast_to((positions < cache_len[request])[:, None, :], (MAXPG, DRAFT, PAGE))
        page_parts = block_partial(jnp.broadcast_to(own_queries[None], (MAXPG, DRAFT, H, HD)), key_rows, value_rows, valid)
        tree_parts = block_partial(own_queries[None], key_new[request][None], value_new[request][None], (reach[request] > 0.5)[None])
        mixture = jnp.concatenate([tree_parts[0], page_parts[0]], axis=0)
        maxima = jnp.concatenate([tree_parts[1], page_parts[1]], axis=0)
        totals = jnp.concatenate([tree_parts[2], page_parts[2]], axis=0)
        return combine_blocks(mixture, maxima, totals)
    attended = lax.map(one_request, jnp.arange(REQS, dtype=jnp.int32))
    attended = attended.reshape(TOKENS, width_all).astype(jnp.bfloat16)
    branch = jnp.dot(attended, w_out, preferred_element_type=jnp.float32)
    normed = layer_norm(hidden_in.astype(jnp.float32) + branch, first_gain).astype(jnp.bfloat16)
    inner = jax.nn.gelu(jnp.dot(normed, w_up, preferred_element_type=jnp.float32), approximate=False).astype(jnp.bfloat16)
    outer = jnp.dot(inner, w_down, preferred_element_type=jnp.float32)
    layer_out = layer_norm(normed.astype(jnp.float32) + outer, second_gain).astype(jnp.bfloat16)
    pairs = jnp.stack([key_new.reshape(REQS, DRAFT, width_all), value_new.reshape(REQS, DRAFT, width_all)], axis=2)
    depth = lax.optimization_barrier(jnp.sum(reach, axis=-1)) - 1.0
    chosen = jnp.einsum('rq,rqk->rk', jax.nn.one_hot(accept_node, DRAFT, dtype=jnp.float32), reach, precision=lax.Precision.HIGHEST)
    levels = jnp.arange(DRAFT, dtype=jnp.float32)
    select = chosen[:, None, :] * (depth[:, None, :] == levels[None, :, None]).astype(jnp.float32)
    accepted_kv = jnp.einsum('rsk,rkcf->rscf', select, pairs.astype(jnp.float32), precision=lax.Precision.HIGHEST).astype(jnp.bfloat16)
    return (layer_out, accepted_kv)
```

```python
import functools

import jax
import jax.numpy as jnp
from jax import lax
from jax.experimental import pallas as pl
from jax.experimental.pallas import tpu as pltpu
from jax.sharding import PartitionSpec as P

HD = 64
NEG = -1e30
EPS = 1e-05
BF = jnp.bfloat16
F32 = jnp.float32
MESH = pl.DeviceIdType.MESH
VMEM_BYTES = 60 * 2**20


def dot(a, b):
    return jnp.dot(a, b, preferred_element_type=F32)


def dot_t(a, b):
    return lax.dot_general(a, b, (((1,), (1,)), ((), ())), preferred_element_type=F32)


def iota(shape, dim):
    return lax.broadcasted_iota(jnp.int32, shape, dim)


def remote(src, dst, ssem, rsem, dev):
    return pltpu.make_async_remote_copy(
        src_ref=src, dst_ref=dst, send_sem=ssem, recv_sem=rsem, device_id=dev, device_id_type=MESH
    )


def greet(devices):
    barrier = pltpu.get_barrier_semaphore()
    for dev in devices:
        pl.semaphore_signal(barrier, inc=1, device_id=dev, device_id_type=MESH)
    pl.semaphore_wait(barrier, len(devices))


def project_kernel(
    sizes,
    hidden,
    weights,
    parents,
    accept,
    lens_row,
    x_out,
    q_out,
    k_out,
    v_out,
    reach_out,
    select_out,
    lens_out,
    xbuf,
    lbuf,
    xs,
    xr,
    ls,
    lr,
):
    n_req, n_tp, pages, chunks = sizes
    e = lax.axis_index("req")
    t = lax.axis_index("tp")
    rows = hidden.shape[0] // chunks
    share = hidden.shape[1]
    peers = [(e, lax.rem(t + r, n_tp)) for r in range(1, n_tp)]
    after = [(lax.rem(e + j, n_req), t) for j in range(1, pages)]
    before = [(lax.rem(e - j + n_req, n_req), t) for j in range(1, pages)]
    greet(peers + after + before)

    def len_copy(j):
        return remote(lens_row, lbuf.at[j - 1], ls.at[j - 1], lr.at[j - 1], after[j - 1])

    def x_copy(r, c):
        span = pl.ds(c * rows, rows)
        return remote(
            hidden.at[span], xbuf.at[r - 1, span], xs.at[r - 1, c], xr.at[r - 1, c], peers[r - 1]
        )

    for j in range(1, pages):
        len_copy(j).start()
    order = [1, 3, 2] if n_tp == 4 else list(range(1, n_tp))
    for c in range(chunks):
        for r in order:
            x_copy(r, c).start()

    requests, draft = parents.shape
    per = 256 // draft
    wide = per * draft
    for g in range(requests // per):
        line = jnp.concatenate(
            [
                jnp.where(parents[g * per + b : g * per + b + 1, :] < 0, -1, parents[g * per + b : g * per + b + 1, :] + b * draft)
                for b in range(per)
            ],
            axis=1,
        )
        low = iota((wide, wide), 0)
        high = iota((wide, wide), 1)
        up = jnp.where((low == line) | (low == high), 1.0, 0.0)
        steps = max(1, (draft - 1).bit_length())
        for _ in range(steps - 1):
            up = jnp.minimum(dot(up.astype(BF), up.astype(BF)), 1.0)
        last = up.astype(BF)
        up = jnp.minimum(dot(last, last), 1.0)
        down = jnp.swapaxes(up, 0, 1)
        depth = jnp.sum(up, axis=0, keepdims=True) - 1.0
        hit = low == -1
        for b in range(per):
            hit = hit | (low == accept[g * per + b] + b * draft)
        chosen = jnp.sum(jnp.where(hit, down, 0.0), axis=0, keepdims=True)
        level = iota((draft, wide), 0).astype(F32)
        select = jnp.where(level == depth, chosen, 0.0)
        select_out[g] = select.astype(BF)
        for b in range(per):
            span = slice(b * draft, (b + 1) * draft)
            reach_out[g * per + b] = down[span, span]

    for c in range(chunks):
        span = pl.ds(c * rows, rows)
        x_out[span, pl.ds(pl.multiple_of(t * share, share), share)] = hidden[span]
        for r in range(1, n_tp):
            x_copy(r, c).wait_recv()
            s = lax.rem(t - r + n_tp, n_tp)
            x_out[span, pl.ds(pl.multiple_of(s * share, share), share)] = xbuf[r - 1, span]
        x = x_out[span]
        both = (dot(x, weights[0]) * 0.125).astype(BF)
        for i in range(rows // draft):
            q_out[c * rows // draft + i] = both[i * draft : (i + 1) * draft]
        k_out[span] = dot(x, weights[1]).astype(BF)
        v_out[span] = dot(x, weights[2]).astype(BF)

    for j in range(1, pages):
        len_copy(j).wait_recv()
    lens_out[...] = lbuf[...]
    for j in range(1, pages):
        len_copy(j).wait_send()
    for c in range(chunks):
        for r in range(1, n_tp):
            x_copy(r, c).wait_send()


def project(sizes, hidden, weights, parents, accept, lens_row):
    n_req, n_tp, pages, chunks = sizes
    tokens, share = hidden.shape
    requests, draft = parents.shape
    width = weights.shape[2]
    vm = pl.BlockSpec(memory_space=pltpu.VMEM)
    sm = pl.BlockSpec(memory_space=pltpu.SMEM)
    sds = jax.ShapeDtypeStruct
    return pl.pallas_call(
        functools.partial(project_kernel, sizes),
        out_shape=(
            sds((tokens, share * n_tp), BF),
            sds((requests, draft, width), BF),
            sds((tokens, width), BF),
            sds((tokens, width), BF),
            sds((requests, draft, draft), F32),
            sds((requests * draft // 256, draft, 256), BF),
            sds((pages - 1, 1, 128), jnp.int32),
        ),
        in_specs=[vm, vm, vm, sm, vm],
        out_specs=(vm,) * 7,
        scratch_shapes=[
            pltpu.VMEM((n_tp - 1, tokens, share), BF),
            pltpu.VMEM((pages - 1, 1, 128), jnp.int32),
            pltpu.SemaphoreType.DMA((n_tp - 1, chunks)),
            pltpu.SemaphoreType.DMA((n_tp - 1, chunks)),
            pltpu.SemaphoreType.DMA((pages - 1,)),
            pltpu.SemaphoreType.DMA((pages - 1,)),
        ],
        compiler_params=pltpu.CompilerParams(
            collective_id=0, has_side_effects=True, vmem_limit_bytes=VMEM_BYTES
        ),
        name="gather_project",
    )(hidden, weights, parents, accept, lens_row)


def diagonal(rows64, mask):
    return jnp.concatenate([rows64] * 4, axis=0) * mask


def fold(wide, draft):
    lane = iota((draft, wide.shape[1]), 1)
    out = wide[0:draft]
    for h in range(1, wide.shape[1] // HD):
        out = jnp.where(lane >= h * HD, wide[h * draft : (h + 1) * draft], out)
    return out


def page_part(queries, page, count, draft):
    scores = pltpu.roll(dot_t(queries, page), 1, 1)
    lane = iota(scores.shape, 1)
    valid = (lane < 2 * count) & (lax.rem(lane, 2) == 1)
    top = jnp.max(jnp.where(valid, scores, NEG), axis=1, keepdims=True)
    weights = jnp.where(valid, jnp.exp(scores - top), 0.0).astype(BF)
    total = jnp.sum(weights.astype(F32), axis=1, keepdims=True)
    return fold(dot(weights, page), draft), top, total


def spread(column, draft):
    lane = iota((draft, 128), 1)
    tiles = []
    for i in range(2):
        a = jnp.broadcast_to(column[2 * i * draft : (2 * i + 1) * draft], (draft, 128))
        b = jnp.broadcast_to(column[(2 * i + 1) * draft : (2 * i + 2) * draft], (draft, 128))
        tiles.append(jnp.where(lane < HD, a, b))
    return jnp.concatenate(tiles, axis=1)


def place(stats, column, at):
    lane = iota(stats.shape, 1)
    return jnp.where(lane == at, column, stats)


def attend_kernel(
    sizes,
    q,
    k,
    v,
    reach,
    select,
    w_own,
    page_table,
    own_len,
    far_len,
    pool,
    att_out,
    kept_k,
    kept_v,
    w_out,
    pages_v,
    qlong,
    q_one,
    q_far,
    part_one,
    stat_one,
    part_far,
    stat_far,
    back_one,
    bstat_one,
    back_far,
    bstat_far,
    acc,
    own_stat,
    wbuf,
    psem,
    q1s,
    q1r,
    qfs,
    qfr,
    p1s,
    p1r,
    t1s,
    t1r,
    pfs,
    pfr,
    tfs,
    tfr,
    ws,
    wr,
    fs,
    fr,
):
    n_req, n_tp, pages, _ = sizes
    e = lax.axis_index("req")
    t = lax.axis_index("tp")
    requests, draft, _ = reach.shape
    page_len = pages_v.shape[1]
    longs = (requests + 3) // 4
    half = w_own.shape[0] // 2
    parity = lax.rem(e, 2)
    partner = (e + 1 - 2 * parity, t)
    peers = [(e, lax.rem(t + r, n_tp)) for r in range(1, n_tp)]

    def ahead(j):
        return (lax.rem(e + j, n_req), t)

    def behind(j):
        return (lax.rem(e - j + n_req, n_req), t)

    load = pltpu.make_async_copy(pool, pages_v, psem)
    load.start()

    def long_pair(length):
        first = jnp.int32(requests)
        second = jnp.int32(0)
        for m in range(requests):
            is_long = length(m) > 2 * page_len
            first = jnp.where(is_long, jnp.minimum(first, m), first)
            second = jnp.where(is_long, jnp.maximum(second, m), second)
        return jnp.minimum(first, requests - 1), second

    mine = long_pair(lambda m: own_len[m])
    for i in range(longs):
        qlong[i] = q[mine[i]]

    greet(peers + [ahead(j) for j in range(1, pages)] + [behind(j) for j in range(1, pages)])

    quarters = requests // 2

    def far_q(j):
        return remote(qlong, q_far.at[j - 2], qfs.at[j - 2], qfr.at[j - 2], ahead(j))

    def one_q(c):
        span = pl.ds(2 * c, 2)
        return remote(q.at[span], q_one.at[span], q1s.at[c], q1r.at[c], ahead(1))

    def one_part(c):
        return remote(part_one.at[c], back_one.at[c], p1s.at[c], p1r.at[c], behind(1))

    def one_stat():
        return remote(stat_one, bstat_one, t1s, t1r, behind(1))

    def far_part(j):
        return remote(part_far.at[j - 2], back_far.at[j - 2], pfs.at[j - 2], pfr.at[j - 2], behind(j))

    def far_stat(j):
        return remote(stat_far.at[j - 2], bstat_far.at[j - 2], tfs.at[j - 2], tfr.at[j - 2], behind(j))

    def w_copy(r):
        return remote(
            w_own.at[pl.ds(pl.multiple_of(parity * half, half), half)],
            wbuf.at[r - 1, parity],
            ws.at[r - 1],
            wr.at[r - 1],
            peers[r - 1],
        )

    def w_pass(r):
        return remote(wbuf.at[r - 1, parity], wbuf.at[r - 1, parity], fs.at[r - 1], fr.at[r - 1], partner)

    for j in range(pages - 1, 1, -1):
        far_q(j).start()
    for c in range(quarters):
        one_q(c).start()
    for r in range(1, n_tp):
        w_copy(r).start()

    width = q.shape[2]
    mask = jnp.where(
        iota((4 * draft, width), 0) // draft == iota((4 * draft, width), 1) // HD, 1.0, 0.0
    ).astype(BF)

    load.wait()

    def page_of(slot):
        return pages_v[slot].reshape(2 * page_len, width)

    for r in range(requests):
        rows = slice(r * draft, (r + 1) * draft)
        queries = diagonal(q[r], mask)
        part, top, total = page_part(queries, page_of(page_table[0, r]), own_len[r], draft)
        allowed = jnp.concatenate([reach[r]] * 4, axis=0) > 0.5
        scores = dot_t(queries, k[rows])
        tree_top = jnp.max(jnp.where(allowed, scores, NEG), axis=1, keepdims=True)
        best = jnp.maximum(top, tree_top)
        weights = jnp.where(allowed, jnp.exp(scores - best), 0.0).astype(BF)
        scale = jnp.exp(top - best)
        total = total * scale + jnp.sum(weights.astype(F32), axis=1, keepdims=True)
        tree = fold(dot(weights, v[rows]), draft)
        acc[r] = part * spread(scale, draft) + tree
        own_stat[r] = place(place(jnp.zeros((4 * draft, 128), F32), best, 0), total, 1)

    for j in range(pages - 1, 1, -1):
        pair = long_pair(lambda m: far_len[j - 1, 0, m])
        far_q(j).wait_recv()
        stats = jnp.zeros((4 * draft, 128), F32)
        for i in range(longs):
            slot = page_table[j, 0]
            count = far_len[j - 1, 0, 0]
            for m in range(1, requests):
                slot = jnp.where(pair[i] == m, page_table[j, m], slot)
                count = jnp.where(pair[i] == m, far_len[j - 1, 0, m], count)
            count = count - j * page_len
            queries = diagonal(q_far[j - 2, i], mask)
            part, top, total = page_part(queries, page_of(slot), count, draft)
            part_far[j - 2, i * draft : (i + 1) * draft] = part.astype(BF)
            stats = place(place(stats, top, 2 * i), total, 2 * i + 1)
        stat_far[j - 2] = jnp.swapaxes(stats, 0, 1)[0:8]
        far_part(j).start()
        far_stat(j).start()

    stats = jnp.zeros((4 * draft, 128), F32)
    for c in range(quarters):
        one_q(c).wait_recv()
        for i in range(2):
            r = 2 * c + i
            count = far_len[0, 0, r] - page_len
            queries = diagonal(q_one[r], mask)
            part, top, total = page_part(queries, page_of(page_table[1, r]), count, draft)
            part_one[c, i * draft : (i + 1) * draft] = part.astype(BF)
            stats = place(place(stats, top, 2 * r), total, 2 * r + 1)
        one_part(c).start()
    stat_one[...] = jnp.swapaxes(stats, 0, 1)[0:16]
    one_stat().start()

    for r in range(1, n_tp):
        w_copy(r).wait_recv()
        w_pass(r).start()

    per = 256 // draft
    for r in range(requests):
        rows = slice(r * draft, (r + 1) * draft)
        b = r % per
        pick = select[r // per][:, b * draft : (b + 1) * draft]
        kept_k[r] = dot(pick, k[rows]).astype(BF)
        kept_v[r] = dot(pick, v[rows]).astype(BF)

    for j in range(pages - 1, 1, -1):
        far_stat(j).wait_recv()
    far_columns = jnp.swapaxes(
        jnp.concatenate(
            [bstat_far[j - 2] for j in range(2, pages)]
            + [jnp.zeros((128 - 8 * (pages - 2), 4 * draft), F32)],
            axis=0,
        ),
        0,
        1,
    )
    for j in range(pages - 1, 1, -1):
        far_part(j).wait_recv()
    long_acc = []
    long_top = []
    long_total = []
    for i in range(longs):
        tops = [far_columns[:, 8 * (j - 2) + 2 * i : 8 * (j - 2) + 2 * i + 1] for j in range(2, pages)]
        sums = [far_columns[:, 8 * (j - 2) + 2 * i + 1 : 8 * (j - 2) + 2 * i + 2] for j in range(2, pages)]
        best = functools.reduce(jnp.maximum, tops)
        total = jnp.zeros_like(best)
        out = jnp.zeros((draft, width), F32)
        for j in range(2, pages):
            scale = jnp.exp(tops[j - 2] - best)
            total = total + scale * sums[j - 2]
            out = out + spread(scale, draft) * back_far[j - 2, i * draft : (i + 1) * draft].astype(F32)
        long_acc.append(out)
        long_top.append(best)
        long_total.append(total)

    one_stat().wait_recv()
    one_columns = jnp.swapaxes(
        jnp.concatenate([bstat_one[...], jnp.zeros((128 - 16, 4 * draft), F32)], axis=0), 0, 1
    )
    for c in range(quarters):
        one_part(c).wait_recv()
        for i in range(2):
            r = 2 * c + i
            tall = (4 * draft, 1)
            second = jnp.full(tall, mine[1], jnp.int32) == r
            is_long = jnp.full(tall, own_len[r], jnp.int32) > 2 * page_len
            top_l = jnp.where(is_long, jnp.where(second, long_top[1], long_top[0]), NEG)
            total_l = jnp.where(second, long_total[1], long_total[0])
            acc_l = jnp.where(
                jnp.full((draft, width), mine[1], jnp.int32) == r, long_acc[1], long_acc[0]
            )
            stat = own_stat[r]
            top_o = stat[:, 0:1]
            total_o = stat[:, 1:2]
            top_1 = one_columns[:, 2 * r : 2 * r + 1]
            total_1 = one_columns[:, 2 * r + 1 : 2 * r + 2]
            best = jnp.maximum(jnp.maximum(top_o, top_1), top_l)
            s_o = jnp.exp(top_o - best)
            s_1 = jnp.exp(top_1 - best)
            s_l = jnp.exp(top_l - best)
            whole = 1.0 / (s_o * total_o + s_1 * total_1 + s_l * total_l)
            out = acc[r] * spread(s_o * whole, draft)
            out = out + back_one[c, i * draft : (i + 1) * draft].astype(F32) * spread(s_1 * whole, draft)
            out = out + acc_l * spread(s_l * whole, draft)
            att_out[r * draft : (r + 1) * draft] = out.astype(BF)

    for r in range(1, n_tp):
        remote(
            wbuf.at[r - 1, 1 - parity], wbuf.at[r - 1, 1 - parity], fs.at[r - 1], fr.at[r - 1], partner
        ).wait_recv()
        for h in range(2):
            w_out[r - 1, h * half : (h + 1) * half] = wbuf[r - 1, h]

    for j in range(2, pages):
        far_q(j).wait_send()
        far_part(j).wait_send()
        far_stat(j).wait_send()
    for c in range(quarters):
        one_q(c).wait_send()
        one_part(c).wait_send()
    one_stat().wait_send()
    for r in range(1, n_tp):
        w_copy(r).wait_send()
        w_pass(r).wait_send()


def attend(sizes, q, k, v, reach, select, w_own, page_table, own_len, far_len, pool):
    n_req, n_tp, pages, _ = sizes
    requests, draft, width = q.shape
    tokens = requests * draft
    slots, page_len = pool.shape[0], pool.shape[1]
    rows_w, cols_w = w_own.shape
    quarters = requests // 2
    far = pages - 2
    vm = pl.BlockSpec(memory_space=pltpu.VMEM)
    sm = pl.BlockSpec(memory_space=pltpu.SMEM)
    sds = jax.ShapeDtypeStruct
    dma = pltpu.SemaphoreType.DMA
    return pl.pallas_call(
        functools.partial(attend_kernel, sizes),
        out_shape=(
            sds((tokens, width), BF),
            sds((requests, draft, width), BF),
            sds((requests, draft, width), BF),
            sds((n_tp - 1, rows_w, cols_w), BF),
        ),
        in_specs=[vm, vm, vm, vm, vm, vm, sm, sm, sm, pl.BlockSpec(memory_space=pl.ANY)],
        out_specs=(vm,) * 4,
        scratch_shapes=[
            pltpu.VMEM((slots, page_len, 2, width), BF),
            pltpu.VMEM((2, draft, width), BF),
            pltpu.VMEM((requests, draft, width), BF),
            pltpu.VMEM((far, 2, draft, width), BF),
            pltpu.VMEM((quarters, 2 * draft, width), BF),
            pltpu.VMEM((16, 4 * draft), F32),
            pltpu.VMEM((far, 2 * draft, width), BF),
            pltpu.VMEM((far, 8, 4 * draft), F32),
            pltpu.VMEM((quarters, 2 * draft, width), BF),
            pltpu.VMEM((16, 4 * draft), F32),
            pltpu.VMEM((far, 2 * draft, width), BF),
            pltpu.VMEM((far, 8, 4 * draft), F32),
            pltpu.VMEM((requests, draft, width), F32),
            pltpu.VMEM((requests, 4 * draft, 128), F32),
            pltpu.VMEM((n_tp - 1, 2, rows_w // 2, cols_w), BF),
            dma,
            dma((quarters,)),
            dma((quarters,)),
            dma((far,)),
            dma((far,)),
            dma((quarters,)),
            dma((quarters,)),
            dma,
            dma,
            dma((far,)),
            dma((far,)),
            dma((far,)),
            dma((far,)),
            dma((n_tp - 1,)),
            dma((n_tp - 1,)),
            dma((n_tp - 1,)),
            dma((n_tp - 1,)),
        ],
        compiler_params=pltpu.CompilerParams(
            collective_id=1, has_side_effects=True, vmem_limit_bytes=VMEM_BYTES
        ),
        name="attend",
    )(q, k, v, reach, select, w_own, page_table, own_len, far_len, pool)


def finish_kernel(
    sizes,
    att,
    x,
    w_own,
    w_far,
    w_up,
    w_down,
    gain1,
    gain2,
    out,
    abuf,
    normed_v,
    share_v,
    obuf,
    rbuf,
    second,
    srow,
    sbuf,
    as_,
    ar,
    os_,
    or_,
    ss,
    sr,
):
    n_req, n_tp, pages, chunks = sizes
    e = lax.axis_index("req")
    t = lax.axis_index("tp")
    tokens, share = att.shape
    rows = tokens // chunks
    width = x.shape[1]
    peers = [(e, lax.rem(t + r, n_tp)) for r in range(1, n_tp)]
    greet(peers)

    def a_copy(r, c):
        span = pl.ds(c * rows, rows)
        return remote(
            att.at[span], abuf.at[r - 1, span], as_.at[r - 1, c], ar.at[r - 1, c], peers[r - 1]
        )

    def o_copy(r, c):
        s = lax.rem(t + r, n_tp)
        span = pl.ds(c * rows, rows)
        return remote(
            obuf.at[span, pl.ds(pl.multiple_of(s * share, share), share)],
            rbuf.at[r - 1, span],
            os_.at[r - 1, c],
            or_.at[r - 1, c],
            peers[r - 1],
        )

    def s_copy(r):
        return remote(srow, sbuf.at[r - 1], ss.at[r - 1], sr.at[r - 1], peers[r - 1])

    order = [1, 3, 2] if n_tp == 4 else list(range(1, n_tp))
    for c in range(chunks):
        for r in order:
            a_copy(r, c).start()

    mine = pl.ds(pl.multiple_of(t * share, share), share)
    for c in range(chunks):
        span = pl.ds(c * rows, rows)
        branch = dot(att[span], w_own[...])
        for r in range(1, n_tp):
            a_copy(r, c).wait_recv()
            branch = branch + dot(abuf[r - 1, span], w_far[r - 1])
        z = x[span].astype(F32) + branch
        center = jnp.sum(z, axis=1, keepdims=True) / width
        var = jnp.sum(z * z, axis=1, keepdims=True) / width - center * center
        normed = ((z - center) * lax.rsqrt(var + EPS) * gain1[...]).astype(BF)
        normed_v[...] = normed
        share_v[span] = normed_v[:, mine]
        pre = dot(normed, w_up[...])
        inner = (0.5 * pre * (1.0 + lax.erf(pre * 0.7071067811865476))).astype(BF)
        obuf[span] = dot(inner, w_down[...]).astype(BF)
        for r in order:
            o_copy(r, c).start()

    lane = iota((rows, 128), 1)
    stats = jnp.zeros((rows, 128), F32)
    for c in range(chunks):
        span = pl.ds(c * rows, rows)
        y = share_v[span].astype(F32) + obuf[span, mine].astype(F32)
        for r in range(1, n_tp):
            o_copy(r, c).wait_recv()
            y = y + rbuf[r - 1, span].astype(F32)
        second[span] = y
        stats = jnp.where(lane == 2 * c, jnp.sum(y, axis=1, keepdims=True), stats)
        stats = jnp.where(lane == 2 * c + 1, jnp.sum(y * y, axis=1, keepdims=True), stats)
    total = jnp.swapaxes(stats, 0, 1)[0:8]
    srow[...] = total
    for r in order:
        s_copy(r).start()
    for r in range(1, n_tp):
        s_copy(r).wait_recv()
        total = total + sbuf[r - 1]
    columns = jnp.swapaxes(
        jnp.concatenate([total, jnp.zeros((128 - 8, rows), F32)], axis=0), 0, 1
    )
    for c in range(chunks):
        span = pl.ds(c * rows, rows)
        center = columns[:, 2 * c : 2 * c + 1] / width
        var = columns[:, 2 * c + 1 : 2 * c + 2] / width - center * center
        out[span] = ((second[span] - center) * lax.rsqrt(var + EPS) * gain2[:, mine]).astype(BF)

    for r in range(1, n_tp):
        s_copy(r).wait_send()
        for c in range(chunks):
            a_copy(r, c).wait_send()
            o_copy(r, c).wait_send()


def finish(sizes, att, x, w_own, w_far, w_up, w_down, gain1, gain2):
    n_req, n_tp, pages, chunks = sizes
    tokens, share = att.shape
    width = x.shape[1]
    rows = tokens // chunks
    vm = pl.BlockSpec(memory_space=pltpu.VMEM)
    dma = pltpu.SemaphoreType.DMA
    return pl.pallas_call(
        functools.partial(finish_kernel, sizes),
        out_shape=jax.ShapeDtypeStruct((tokens, share), BF),
        in_specs=[vm] * 8,
        out_specs=vm,
        scratch_shapes=[
            pltpu.VMEM((n_tp - 1, tokens, share), BF),
            pltpu.VMEM((rows, width), BF),
            pltpu.VMEM((tokens, share), BF),
            pltpu.VMEM((tokens, width), BF),
            pltpu.VMEM((n_tp - 1, tokens, share), BF),
            pltpu.VMEM((tokens, share), F32),
            pltpu.VMEM((8, rows), F32),
            pltpu.VMEM((n_tp - 1, 8, rows), F32),
            dma((n_tp - 1, chunks)),
            dma((n_tp - 1, chunks)),
            dma((n_tp - 1, chunks)),
            dma((n_tp - 1, chunks)),
            dma((n_tp - 1,)),
            dma((n_tp - 1,)),
        ],
        compiler_params=pltpu.CompilerParams(
            collective_id=2, has_side_effects=True, vmem_limit_bytes=VMEM_BYTES
        ),
        name="finish",
    )(att, x, w_own, w_far, w_up, w_down, gain1.reshape(1, -1), gain2.reshape(1, -1))


def shards(
    sizes,
    hidden_in,
    w_qkv,
    w_out,
    first_gain,
    w_up,
    w_down,
    second_gain,
    cache_pool,
    page_table,
    cache_len,
    tree_parent,
    accept_node,
):
    requests = tree_parent.shape[0]
    lens_row = jnp.pad(cache_len, (0, 128 - requests)).reshape(1, 128)
    x, q, k, v, reach, select, far_len = project(
        sizes, hidden_in, jnp.transpose(w_qkv, (1, 0, 2)), tree_parent, accept_node, lens_row
    )
    att, kept_k, kept_v, w_far = attend(
        sizes, q, k, v, reach, select, w_out, page_table, cache_len, far_len, cache_pool
    )
    layer_out = finish(sizes, att, x, w_out, w_far, w_up, w_down, first_gain, second_gain)
    return layer_out, jnp.stack([kept_k, kept_v], axis=2)


def solution(mesh):
    placed = (
        P("req", "tp"),
        P(None, None, "tp"),
        P("tp", None),
        P(),
        P(None, "tp"),
        P("tp", None),
        P(),
        P("req", None, None, "tp"),
        P("req", None),
        P("req"),
        P("req", None),
        P("req"),
    )
    sizes = (mesh.shape["req"], mesh.shape["tp"], 8, 4)
    return jax.shard_map(
        functools.partial(shards, sizes),
        mesh=mesh,
        in_specs=placed,
        out_specs=(P("req", "tp"), P("req", None, None, "tp")),
        check_vma=False,
    )
```

```python
import functools

import jax
import jax.numpy as jnp
from jax import lax
from jax.experimental import pallas as pl
from jax.experimental.pallas import tpu as pltpu
from jax.sharding import PartitionSpec as P

HD = 64
NEG = -1e30
EPS = 1e-05
BF = jnp.bfloat16
F32 = jnp.float32
MESH = pl.DeviceIdType.MESH
VMEM_BYTES = 60 * 2**20


def dot(a, b):
    return jnp.dot(a, b, preferred_element_type=F32)


def dot_t(a, b):
    return lax.dot_general(a, b, (((1,), (1,)), ((), ())), preferred_element_type=F32)


def iota(shape, dim):
    return lax.broadcasted_iota(jnp.int32, shape, dim)


def remote(src, dst, ssem, rsem, dev):
    return pltpu.make_async_remote_copy(
        src_ref=src, dst_ref=dst, send_sem=ssem, recv_sem=rsem, device_id=dev, device_id_type=MESH
    )


def greet(devices):
    barrier = pltpu.get_barrier_semaphore()
    for dev in devices:
        pl.semaphore_signal(barrier, inc=1, device_id=dev, device_id_type=MESH)
    pl.semaphore_wait(barrier, len(devices))


def diagonal(rows64, mask):
    return jnp.concatenate([rows64] * 4, axis=0) * mask


def fold(wide, draft):
    lane = iota((draft, wide.shape[1]), 1)
    out = wide[0:draft]
    for h in range(1, wide.shape[1] // HD):
        out = jnp.where(lane >= h * HD, wide[h * draft : (h + 1) * draft], out)
    return out


def page_part(queries, page, count, draft):
    scores = pltpu.roll(dot_t(queries, page), 1, 1)
    lane = iota(scores.shape, 1)
    valid = (lane < 2 * count) & (lax.rem(lane, 2) == 1)
    top = jnp.max(jnp.where(valid, scores, NEG), axis=1, keepdims=True)
    weights = jnp.where(valid, jnp.exp(scores - top), 0.0).astype(BF)
    total = jnp.sum(weights.astype(F32), axis=1, keepdims=True)
    return fold(dot(weights, page), draft), top, total


def spread(column, draft):
    lane = iota((draft, 128), 1)
    tiles = []
    for i in range(2):
        a = jnp.broadcast_to(column[2 * i * draft : (2 * i + 1) * draft], (draft, 128))
        b = jnp.broadcast_to(column[(2 * i + 1) * draft : (2 * i + 2) * draft], (draft, 128))
        tiles.append(jnp.where(lane < HD, a, b))
    return jnp.concatenate(tiles, axis=1)


def place(stats, column, at):
    lane = iota(stats.shape, 1)
    return jnp.where(lane == at, column, stats)


def layer_kernel(
    sizes,
    hidden,
    w_own,
    gain1,
    gain2,
    parents,
    accept,
    page_table,
    own_len,
    qkv_hbm,
    up_hbm,
    down_hbm,
    pool,
    out,
    kept_k,
    kept_v,
    weights,
    w_up,
    w_down,
    pages_v,
    load_sem,
    x_v,
    q,
    k,
    v,
    reach,
    select,
    lens_row,
    lbuf,
    far_len,
    xbuf,
    qlong,
    q_one,
    q_far,
    part_one,
    stat_one,
    part_far,
    stat_far,
    back_one,
    bstat_one,
    back_far,
    bstat_far,
    acc,
    own_stat,
    wbuf,
    att,
    abuf,
    normed_v,
    share_v,
    obuf,
    rbuf,
    second_v,
    srow,
    sbuf,
    xs,
    xr,
    vs,
    vr,
    ls,
    lr,
    q1s,
    q1r,
    qfs,
    qfr,
    p1s,
    p1r,
    t1s,
    t1r,
    pfs,
    pfr,
    tfs,
    tfr,
    ws,
    wr,
    fs,
    fr,
    as_,
    ar,
    bs,
    br,
    os_,
    or_,
    ss,
    sr,
):
    n_req, n_tp, pages, chunks = sizes
    e = lax.axis_index("req")
    t = lax.axis_index("tp")
    tokens, share = hidden.shape
    requests, draft = parents.shape
    rows = tokens // chunks
    step = rows // 2
    width = share
    full = share * n_tp
    page_len = pages_v.shape[1]
    longs = (requests + 3) // 4
    half = w_own.shape[0] // 2
    parity = lax.rem(e, 2)
    partner = (e + 1 - 2 * parity, t)
    peers = [(e, lax.rem(t + r, n_tp)) for r in range(1, n_tp)]
    right, left = peers[0], peers[2]

    def ahead(j):
        return (lax.rem(e + j, n_req), t)

    def behind(j):
        return (lax.rem(e - j + n_req, n_req), t)

    loads = [
        pltpu.make_async_copy(a, b, load_sem.at[i])
        for i, (a, b) in enumerate(
            [(qkv_hbm, weights), (pool, pages_v), (up_hbm, w_up), (down_hbm, w_down)]
        )
    ]
    for load in loads:
        load.start()

    lane_row = iota((1, 128), 1)
    line = jnp.zeros((1, 128), jnp.int32)
    for m in range(requests):
        line = jnp.where(lane_row == m, own_len[m], line)
    lens_row[...] = line

    greet(peers + [ahead(j) for j in range(1, pages)] + [behind(j) for j in range(1, pages)])

    def span_of(c):
        return pl.ds(c * rows, rows)

    def part_of(c, i):
        return pl.ds(c * rows + i * step, step)

    def len_copy(j):
        return remote(lens_row, lbuf.at[j - 1], ls.at[j - 1], lr.at[j - 1], ahead(j))

    def near(source, buf, send, recv, i, c):
        span = span_of(c)
        return remote(
            source.at[span], buf.at[2 * i, span], send.at[i, c], recv.at[i, c], (right, left)[i]
        )

    def onward(buf, send, recv, i, c):
        span = part_of(c, i)
        return remote(
            buf.at[2 * i, span], buf.at[1, span], send.at[i, c], recv.at[i, c], (right, left)[i]
        )

    def x_near(i, c):
        return near(hidden, xbuf, xs, xr, i, c)

    def x_onward(i, c):
        return onward(xbuf, vs, vr, i, c)

    def a_near(i, c):
        return near(att, abuf, as_, ar, i, c)

    def a_onward(i, c):
        return onward(abuf, bs, br, i, c)

    def far_q(j):
        return remote(qlong, q_far.at[j - 2], qfs.at[j - 2], qfr.at[j - 2], ahead(j))

    def one_q(c):
        span = pl.ds(2 * c, 2)
        return remote(q.at[span], q_one.at[span], q1s.at[c], q1r.at[c], ahead(1))

    def one_part(c):
        return remote(part_one.at[c], back_one.at[c], p1s.at[c], p1r.at[c], behind(1))

    def one_stat():
        return remote(stat_one, bstat_one, t1s, t1r, behind(1))

    def far_part(j):
        return remote(part_far.at[j - 2], back_far.at[j - 2], pfs.at[j - 2], pfr.at[j - 2], behind(j))

    def far_stat(j):
        return remote(stat_far.at[j - 2], bstat_far.at[j - 2], tfs.at[j - 2], tfr.at[j - 2], behind(j))

    def w_half(r, which):
        return wbuf.at[r - 1, pl.ds(pl.multiple_of(which * half, half), half)]

    def w_copy(r):
        return remote(
            w_own.at[pl.ds(pl.multiple_of(parity * half, half), half)],
            w_half(r, parity),
            ws.at[r - 1],
            wr.at[r - 1],
            peers[r - 1],
        )

    def w_pass(r, which):
        return remote(w_half(r, which), w_half(r, which), fs.at[r - 1], fr.at[r - 1], partner)

    def o_copy(r, c):
        s = lax.rem(t + r, n_tp)
        span = span_of(c)
        return remote(
            obuf.at[span, pl.ds(pl.multiple_of(s * share, share), share)],
            rbuf.at[r - 1, span],
            os_.at[r - 1, c],
            or_.at[r - 1, c],
            peers[r - 1],
        )

    def s_copy(r):
        return remote(srow, sbuf.at[r - 1], ss.at[r - 1], sr.at[r - 1], peers[r - 1])

    for j in range(1, pages):
        len_copy(j).start()
    for c in range(chunks):
        for i in range(2):
            x_near(i, c).start()

    per = 256 // draft
    wide = per * draft

    def ancestors(g):
        line = jnp.concatenate(
            [
                jnp.where(
                    parents[g * per + b : g * per + b + 1, :] < 0,
                    -1,
                    parents[g * per + b : g * per + b + 1, :] + b * draft,
                )
                for b in range(per)
            ],
            axis=1,
        )
        low = iota((wide, wide), 0)
        high = iota((wide, wide), 1)
        up = jnp.where((low == line) | (low == high), 1.0, 0.0)
        steps = max(1, (draft - 1).bit_length())
        for _ in range(steps):
            last = up.astype(BF)
            up = jnp.minimum(dot(last, last), 1.0)
        down = jnp.swapaxes(up, 0, 1)
        depth = jnp.sum(up, axis=0, keepdims=True) - 1.0
        hit = low == -1
        for b in range(per):
            hit = hit | (low == accept[g * per + b] + b * draft)
        chosen = jnp.sum(jnp.where(hit, down, 0.0), axis=0, keepdims=True)
        level = iota((draft, wide), 0).astype(F32)
        select[g] = jnp.where(level == depth, chosen, 0.0).astype(BF)
        for b in range(per):
            span = slice(b * draft, (b + 1) * draft)
            reach[g * per + b] = down[span, span]

    def x_arrive(c):
        for i in range(2):
            x_near(i, c).wait_recv()
            x_onward(i, c).start()

    groups = requests // per
    ancestors(0)
    for c in range(chunks // 2):
        x_arrive(c)
    for g in range(1, groups):
        ancestors(g)
    for c in range(chunks // 2, chunks):
        x_arrive(c)

    def columns_of(s):
        return pl.ds(pl.multiple_of(s * share, share), share)

    loads[0].wait()
    for c in range(chunks):
        span = span_of(c)
        x_v[span, columns_of(t)] = hidden[span]
        for r in (1, 3):
            x_v[span, columns_of(lax.rem(t - r + n_tp, n_tp))] = xbuf[r - 1, span]
        for i in range(2):
            x_onward(i, c).wait_recv()
        x_v[span, columns_of(lax.rem(t - 2 + n_tp, n_tp))] = xbuf[1, span]
        x = x_v[span]
        both = (dot(x, weights[0]) * 0.125).astype(BF)
        for i in range(rows // draft):
            q[c * rows // draft + i] = both[i * draft : (i + 1) * draft]
        one_q(c).start()
        k[span] = dot(x, weights[1]).astype(BF)
        v[span] = dot(x, weights[2]).astype(BF)

    def long_pair(length):
        first = jnp.int32(requests)
        second = jnp.int32(0)
        for m in range(requests):
            is_long = length(m) > 2 * page_len
            first = jnp.where(is_long, jnp.minimum(first, m), first)
            second = jnp.where(is_long, jnp.maximum(second, m), second)
        return jnp.minimum(first, requests - 1), second

    mine = long_pair(lambda m: own_len[m])
    for i in range(longs):
        qlong[i] = q[mine[i]]
    for j in range(pages - 1, 1, -1):
        far_q(j).start()
    for r in range(1, n_tp):
        w_copy(r).start()

    for j in range(1, pages):
        len_copy(j).wait_recv()
    lens_in = pltpu.make_async_copy(lbuf, far_len, load_sem.at[4])
    lens_in.start()

    mask = jnp.where(
        iota((4 * draft, width), 0) // draft == iota((4 * draft, width), 1) // HD, 1.0, 0.0
    ).astype(BF)

    loads[1].wait()
    lens_in.wait()

    def page_of(slot):
        return pages_v[slot].reshape(2 * page_len, width)

    stats = jnp.zeros((4 * draft, 128), F32)
    for c in range(chunks):
        one_q(c).wait_recv()
        for i in range(2):
            r = 2 * c + i
            count = far_len[0, 0, r] - page_len
            queries = diagonal(q_one[r], mask)
            part, top, total = page_part(queries, page_of(page_table[1, r]), count, draft)
            part_one[c, i * draft : (i + 1) * draft] = part.astype(BF)
            stats = place(place(stats, top, 2 * r), total, 2 * r + 1)
        one_part(c).start()
    stat_one[...] = jnp.swapaxes(stats, 0, 1)[0:16]
    one_stat().start()

    for j in range(pages - 1, 1, -1):
        pair = long_pair(lambda m: far_len[j - 1, 0, m])
        far_q(j).wait_recv()
        stats = jnp.zeros((4 * draft, 128), F32)
        for i in range(longs):
            slot = page_table[j, 0]
            count = far_len[j - 1, 0, 0]
            for m in range(1, requests):
                slot = jnp.where(pair[i] == m, page_table[j, m], slot)
                count = jnp.where(pair[i] == m, far_len[j - 1, 0, m], count)
            count = count - j * page_len
            queries = diagonal(q_far[j - 2, i], mask)
            part, top, total = page_part(queries, page_of(slot), count, draft)
            part_far[j - 2, i * draft : (i + 1) * draft] = part.astype(BF)
            stats = place(place(stats, top, 2 * i), total, 2 * i + 1)
        stat_far[j - 2] = jnp.swapaxes(stats, 0, 1)[0:8]
        far_part(j).start()
        far_stat(j).start()

    for r in range(1, n_tp):
        w_copy(r).wait_recv()
        w_pass(r, parity).start()

    def own(r):
        span = slice(r * draft, (r + 1) * draft)
        queries = diagonal(q[r], mask)
        part, top, total = page_part(queries, page_of(page_table[0, r]), own_len[r], draft)
        allowed = jnp.concatenate([reach[r]] * 4, axis=0) > 0.5
        scores = dot_t(queries, k[span])
        tree_top = jnp.max(jnp.where(allowed, scores, NEG), axis=1, keepdims=True)
        best = jnp.maximum(top, tree_top)
        weight = jnp.where(allowed, jnp.exp(scores - best), 0.0).astype(BF)
        scale = jnp.exp(top - best)
        total = total * scale + jnp.sum(weight.astype(F32), axis=1, keepdims=True)
        tree = fold(dot(weight, v[span]), draft)
        acc[r] = part * spread(scale, draft) + tree
        own_stat[r] = place(place(jnp.zeros((4 * draft, 128), F32), best, 0), total, 1)

    def long_parts():
        for j in range(pages - 1, 1, -1):
            far_stat(j).wait_recv()
            far_part(j).wait_recv()
        far_columns = jnp.swapaxes(
            jnp.concatenate(
                [bstat_far[j - 2] for j in range(2, pages)]
                + [jnp.zeros((128 - 8 * (pages - 2), 4 * draft), F32)],
                axis=0,
            ),
            0,
            1,
        )
        found = []
        for i in range(longs):
            at = [8 * (j - 2) + 2 * i for j in range(2, pages)]
            tops = [far_columns[:, a : a + 1] for a in at]
            sums = [far_columns[:, a + 1 : a + 2] for a in at]
            best = functools.reduce(jnp.maximum, tops)
            total = jnp.zeros_like(best)
            whole = jnp.zeros((draft, width), F32)
            for j in range(2, pages):
                scale = jnp.exp(tops[j - 2] - best)
                total = total + scale * sums[j - 2]
                part = back_far[j - 2, i * draft : (i + 1) * draft].astype(F32)
                whole = whole + spread(scale, draft) * part
            found.append((whole, best, total))
        return found

    def combine(c, found, one_columns):
        one_part(c).wait_recv()
        for i in range(2):
            r = 2 * c + i
            tall = (4 * draft, 1)
            later = jnp.full(tall, mine[1], jnp.int32) == r
            is_long = jnp.full(tall, own_len[r], jnp.int32) > 2 * page_len
            top_l = jnp.where(is_long, jnp.where(later, found[1][1], found[0][1]), NEG)
            total_l = jnp.where(later, found[1][2], found[0][2])
            acc_l = jnp.where(
                jnp.full((draft, width), mine[1], jnp.int32) == r, found[1][0], found[0][0]
            )
            stat = own_stat[r]
            top_o = stat[:, 0:1]
            total_o = stat[:, 1:2]
            top_1 = one_columns[:, 2 * r : 2 * r + 1]
            total_1 = one_columns[:, 2 * r + 1 : 2 * r + 2]
            best = jnp.maximum(jnp.maximum(top_o, top_1), top_l)
            s_o = jnp.exp(top_o - best)
            s_1 = jnp.exp(top_1 - best)
            s_l = jnp.exp(top_l - best)
            whole = 1.0 / (s_o * total_o + s_1 * total_1 + s_l * total_l)
            y = acc[r] * spread(s_o * whole, draft)
            y = y + back_one[c, i * draft : (i + 1) * draft].astype(F32) * spread(s_1 * whole, draft)
            y = y + acc_l * spread(s_l * whole, draft)
            att[r * draft : (r + 1) * draft] = y.astype(BF)
        for i in range(2):
            a_near(i, c).start()

    def a_arrive(c):
        for i in range(2):
            a_near(i, c).wait_recv()
            a_onward(i, c).start()

    for r in range(4):
        own(r)
    found = long_parts()
    one_stat().wait_recv()
    one_columns = jnp.swapaxes(
        jnp.concatenate([bstat_one[...], jnp.zeros((128 - 16, 4 * draft), F32)], axis=0), 0, 1
    )
    for c in range(chunks):
        combine(c, found, one_columns)
        if c > 0:
            a_arrive(c - 1)
        if c + 2 < chunks:
            own(2 * c + 4)
            own(2 * c + 5)

    for r in range(1, n_tp):
        w_pass(r, 1 - parity).wait_recv()
    loads[2].wait()
    loads[3].wait()
    order = [1, 3, 2]
    mine_cols = columns_of(t)
    for c in range(chunks):
        span = span_of(c)
        branch = dot(att[span], w_own[...])
        if c == 0:
            a_arrive(chunks - 1)
        for r in (1, 3):
            branch = branch + dot(abuf[r - 1, span], wbuf[r - 1])
        for i in range(2):
            a_onward(i, c).wait_recv()
        branch = branch + dot(abuf[1, span], wbuf[1])
        z = x_v[span].astype(F32) + branch
        center = jnp.sum(z, axis=1, keepdims=True) / full
        var = jnp.sum(z * z, axis=1, keepdims=True) / full - center * center
        normed = ((z - center) * lax.rsqrt(var + EPS) * gain1[...]).astype(BF)
        normed_v[...] = normed
        share_v[span] = normed_v[:, mine_cols]
        pre = dot(normed, w_up[...])
        inner = (0.5 * pre * (1.0 + lax.erf(pre * 0.7071067811865476))).astype(BF)
        obuf[span] = dot(inner, w_down[...]).astype(BF)
        for r in order:
            o_copy(r, c).start()

    for r in range(requests):
        span = slice(r * draft, (r + 1) * draft)
        b = r % per
        pick = select[r // per][:, b * draft : (b + 1) * draft]
        kept_k[r] = dot(pick, k[span]).astype(BF)
        kept_v[r] = dot(pick, v[span]).astype(BF)

    lane = iota((rows, 128), 1)
    stats = jnp.zeros((rows, 128), F32)
    for c in range(chunks):
        span = span_of(c)
        y = share_v[span].astype(F32) + obuf[span, mine_cols].astype(F32)
        for r in range(1, n_tp):
            o_copy(r, c).wait_recv()
            y = y + rbuf[r - 1, span].astype(F32)
        second_v[span] = y
        stats = jnp.where(lane == 2 * c, jnp.sum(y, axis=1, keepdims=True), stats)
        stats = jnp.where(lane == 2 * c + 1, jnp.sum(y * y, axis=1, keepdims=True), stats)
    total = jnp.swapaxes(stats, 0, 1)[0:8]
    srow[...] = total
    for r in order:
        s_copy(r).start()
    for r in range(1, n_tp):
        s_copy(r).wait_recv()
        total = total + sbuf[r - 1]
    columns = jnp.swapaxes(
        jnp.concatenate([total, jnp.zeros((128 - 8, rows), F32)], axis=0), 0, 1
    )
    for c in range(chunks):
        span = span_of(c)
        center = columns[:, 2 * c : 2 * c + 1] / full
        var = columns[:, 2 * c + 1 : 2 * c + 2] / full - center * center
        out[span] = ((second_v[span] - center) * lax.rsqrt(var + EPS) * gain2[:, mine_cols]).astype(BF)

    for j in range(1, pages):
        len_copy(j).wait_send()
    for j in range(2, pages):
        far_q(j).wait_send()
        far_part(j).wait_send()
        far_stat(j).wait_send()
    one_stat().wait_send()
    for c in range(chunks):
        one_q(c).wait_send()
        one_part(c).wait_send()
        for i in range(2):
            x_near(i, c).wait_send()
            x_onward(i, c).wait_send()
            a_near(i, c).wait_send()
            a_onward(i, c).wait_send()
    for r in range(1, n_tp):
        w_copy(r).wait_send()
        w_pass(r, parity).wait_send()
        s_copy(r).wait_send()
        for c in range(chunks):
            o_copy(r, c).wait_send()


def layer(
    sizes, hidden, w_own, gain1, gain2, parents, accept, page_table, own_len, w_qkv, w_up, w_down, pool
):
    n_req, n_tp, pages, chunks = sizes
    tokens, share = hidden.shape
    requests, draft = parents.shape
    full = share * n_tp
    rows = tokens // chunks
    far = pages - 2
    others = n_tp - 1
    vm = pl.BlockSpec(memory_space=pltpu.VMEM)
    sm = pl.BlockSpec(memory_space=pltpu.SMEM)
    hbm = pl.BlockSpec(memory_space=pl.ANY)
    sds = jax.ShapeDtypeStruct
    dma = pltpu.SemaphoreType.DMA
    vmem = pltpu.VMEM
    pairs = [dma(s) for s in [(2, chunks), (2, chunks), (pages - 1,), (chunks,), (far,), (chunks,)] for _ in range(2)]
    pairs += [dma, dma]
    pairs += [
        dma(s)
        for s in [(far,), (far,), (others,), (others,), (2, chunks), (2, chunks), (others, chunks), (others,)]
        for _ in range(2)
    ]
    return pl.pallas_call(
        functools.partial(layer_kernel, sizes),
        out_shape=(
            sds((tokens, share), BF),
            sds((requests, draft, share), BF),
            sds((requests, draft, share), BF),
        ),
        in_specs=[vm, vm, vm, vm, vm, sm, sm, sm, hbm, hbm, hbm, hbm],
        out_specs=(vm,) * 3,
        scratch_shapes=[
            vmem(w_qkv.shape, BF),
            vmem(w_up.shape, BF),
            vmem(w_down.shape, BF),
            vmem(pool.shape, BF),
            dma((5,)),
            vmem((tokens, full), BF),
            vmem((requests, draft, share), BF),
            vmem((tokens, share), BF),
            vmem((tokens, share), BF),
            vmem((requests, draft, draft), F32),
            vmem((requests * draft // 256, draft, 256), BF),
            vmem((1, 128), jnp.int32),
            vmem((pages - 1, 1, 128), jnp.int32),
            pltpu.SMEM((pages - 1, 1, 128), jnp.int32),
            vmem((others, tokens, share), BF),
            vmem((2, draft, share), BF),
            vmem((requests, draft, share), BF),
            vmem((far, 2, draft, share), BF),
            vmem((chunks, 2 * draft, share), BF),
            vmem((16, 4 * draft), F32),
            vmem((far, 2 * draft, share), BF),
            vmem((far, 8, 4 * draft), F32),
            vmem((chunks, 2 * draft, share), BF),
            vmem((16, 4 * draft), F32),
            vmem((far, 2 * draft, share), BF),
            vmem((far, 8, 4 * draft), F32),
            vmem((requests, draft, share), F32),
            vmem((requests, 4 * draft, 128), F32),
            vmem((others,) + w_own.shape, BF),
            vmem((tokens, share), BF),
            vmem((others, tokens, share), BF),
            vmem((rows, full), BF),
            vmem((tokens, share), BF),
            vmem((tokens, full), BF),
            vmem((others, tokens, share), BF),
            vmem((tokens, share), F32),
            vmem((8, rows), F32),
            vmem((others, 8, rows), F32),
        ]
        + pairs,
        compiler_params=pltpu.CompilerParams(
            collective_id=0, has_side_effects=True, vmem_limit_bytes=VMEM_BYTES
        ),
        name="layer",
    )(
        hidden,
        w_own,
        gain1.reshape(1, -1),
        gain2.reshape(1, -1),
        parents,
        accept,
        page_table,
        own_len,
        w_qkv,
        w_up,
        w_down,
        pool,
    )


def shards(
    sizes,
    hidden_in,
    w_qkv,
    w_out,
    first_gain,
    w_up,
    w_down,
    second_gain,
    cache_pool,
    page_table,
    cache_len,
    tree_parent,
    accept_node,
):
    layer_out, kept_k, kept_v = layer(
        sizes,
        hidden_in,
        w_out,
        first_gain,
        second_gain,
        tree_parent,
        accept_node,
        page_table,
        cache_len,
        jnp.transpose(w_qkv, (1, 0, 2)),
        w_up,
        w_down,
        cache_pool,
    )
    return layer_out, jnp.stack([kept_k, kept_v], axis=2)


def solution(mesh):
    placed = (
        P("req", "tp"),
        P(None, None, "tp"),
        P("tp", None),
        P(),
        P(None, "tp"),
        P("tp", None),
        P(),
        P("req", None, None, "tp"),
        P("req", None),
        P("req"),
        P("req", None),
        P("req"),
    )
    sizes = (mesh.shape["req"], mesh.shape["tp"], 8, 4)
    return jax.shard_map(
        functools.partial(shards, sizes),
        mesh=mesh,
        in_specs=placed,
        out_specs=(P("req", "tp"), P("req", None, None, "tp")),
        check_vma=False,
    )
```

```python
import functools

import jax
import jax.numpy as jnp
from jax import lax
from jax.experimental import pallas as pl
from jax.experimental.pallas import tpu as pltpu
from jax.sharding import PartitionSpec as P

HD = 64
NEG = -1e30
EPS = 1e-05
BF = jnp.bfloat16
F32 = jnp.float32
MESH = pl.DeviceIdType.MESH
VMEM_BYTES = 60 * 2**20


def dot(a, b):
    return jnp.dot(a, b, preferred_element_type=F32)


def dot_t(a, b):
    return lax.dot_general(a, b, (((1,), (1,)), ((), ())), preferred_element_type=F32)


def iota(shape, dim):
    return lax.broadcasted_iota(jnp.int32, shape, dim)


def remote(src, dst, ssem, rsem, dev):
    return pltpu.make_async_remote_copy(
        src_ref=src, dst_ref=dst, send_sem=ssem, recv_sem=rsem, device_id=dev, device_id_type=MESH
    )


def greet(devices):
    barrier = pltpu.get_barrier_semaphore()
    for dev in devices:
        pl.semaphore_signal(barrier, inc=1, device_id=dev, device_id_type=MESH)
    pl.semaphore_wait(barrier, len(devices))


def diagonal(rows64, mask):
    return jnp.concatenate([rows64] * 4, axis=0) * mask


def fold(wide, draft):
    lane = iota((draft, wide.shape[1]), 1)
    out = wide[0:draft]
    for h in range(1, wide.shape[1] // HD):
        out = jnp.where(lane >= h * HD, wide[h * draft : (h + 1) * draft], out)
    return out


def page_part(queries, page, count, draft):
    scores = pltpu.roll(dot_t(queries, page), 1, 1)
    lane = iota(scores.shape, 1)
    valid = (lane < 2 * count) & (lax.rem(lane, 2) == 1)
    top = jnp.max(jnp.where(valid, scores, NEG), axis=1, keepdims=True)
    weights = jnp.where(valid, jnp.exp(scores - top), 0.0).astype(BF)
    total = jnp.sum(weights.astype(F32), axis=1, keepdims=True)
    return fold(dot(weights, page), draft), top, total


def spread(column, draft):
    lane = iota((draft, 128), 1)
    tiles = []
    for i in range(2):
        a = jnp.broadcast_to(column[2 * i * draft : (2 * i + 1) * draft], (draft, 128))
        b = jnp.broadcast_to(column[(2 * i + 1) * draft : (2 * i + 2) * draft], (draft, 128))
        tiles.append(jnp.where(lane < HD, a, b))
    return jnp.concatenate(tiles, axis=1)


def place(stats, column, at):
    lane = iota(stats.shape, 1)
    return jnp.where(lane == at, column, stats)


def layer_kernel(
    sizes,
    hidden,
    w_own,
    gain1,
    gain2,
    parents,
    accept,
    page_table,
    own_len,
    qkv_hbm,
    up_hbm,
    down_hbm,
    pool,
    out,
    kept,
    weights,
    w_up,
    w_down,
    pages_v,
    load_sem,
    x_v,
    q,
    k,
    v,
    reach,
    select,
    lens_row,
    lbuf,
    far_len,
    xbuf,
    qlong,
    q_one,
    q_far,
    part_one,
    stat_one,
    part_far,
    stat_far,
    back_one,
    bstat_one,
    back_far,
    bstat_far,
    acc,
    own_stat,
    wbuf,
    att,
    abuf,
    normed_v,
    share_v,
    obuf,
    rbuf,
    second_v,
    done,
    srow,
    sbuf,
    xs,
    xr,
    vs,
    vr,
    ls,
    lr,
    q1s,
    q1r,
    qfs,
    qfr,
    p1s,
    p1r,
    t1s,
    t1r,
    pfs,
    pfr,
    tfs,
    tfr,
    ws,
    wr,
    us,
    ur,
    fs,
    fr,
    as_,
    ar,
    bs,
    br,
    os_,
    or_,
    ss,
    sr,
):
    n_req, n_tp, pages, chunks = sizes
    e = lax.axis_index("req")
    t = lax.axis_index("tp")
    tokens, share = hidden.shape
    requests, draft = parents.shape
    rows = tokens // chunks
    step = rows // 2
    width = share
    full = share * n_tp
    page_len = pages_v.shape[1]
    longs = (requests + 3) // 4
    half = w_own.shape[0] // 2
    parity = lax.rem(e, 2)
    partner = (e + 1 - 2 * parity, t)
    peers = [(e, lax.rem(t + r, n_tp)) for r in range(1, n_tp)]
    right, left = peers[0], peers[2]

    def ahead(j):
        return (lax.rem(e + j, n_req), t)

    def behind(j):
        return (lax.rem(e - j + n_req, n_req), t)

    loads = [
        pltpu.make_async_copy(a, b, load_sem.at[i])
        for i, (a, b) in enumerate(
            [(qkv_hbm, weights), (pool, pages_v), (up_hbm, w_up), (down_hbm, w_down)]
        )
    ]
    for load in loads:
        load.start()

    lane_row = iota((1, 128), 1)
    line = jnp.zeros((1, 128), jnp.int32)
    for m in range(requests):
        line = jnp.where(lane_row == m, own_len[m], line)
    lens_row[...] = line

    greet(peers + [ahead(j) for j in range(1, pages)] + [behind(j) for j in range(1, pages)])

    def span_of(c):
        return pl.ds(c * rows, rows)

    def part_of(c, i):
        return pl.ds(c * rows + i * step, step)

    def len_copy(j):
        return remote(lens_row, lbuf.at[j - 1], ls.at[j - 1], lr.at[j - 1], ahead(j))

    def near(source, buf, send, recv, i, c):
        span = span_of(c)
        return remote(
            source.at[span], buf.at[2 * i, span], send.at[i, c], recv.at[i, c], (right, left)[i]
        )

    def onward(buf, send, recv, i, c):
        span = part_of(c, i)
        return remote(
            buf.at[2 * i, span], buf.at[1, span], send.at[i, c], recv.at[i, c], (right, left)[i]
        )

    def x_near(i, c):
        return near(hidden, xbuf, xs, xr, i, c)

    def x_onward(i, c):
        return onward(xbuf, vs, vr, i, c)

    def a_near(i, c):
        return near(att, abuf, as_, ar, i, c)

    def a_onward(i, c):
        return onward(abuf, bs, br, i, c)

    def far_q(j):
        return remote(qlong, q_far.at[j - 2], qfs.at[j - 2], qfr.at[j - 2], ahead(j))

    def one_q(c):
        span = pl.ds(2 * c, 2)
        return remote(q.at[span], q_one.at[span], q1s.at[c], q1r.at[c], ahead(1))

    def one_part(c):
        span = pl.ds(2 * c, 2)
        return remote(part_one.at[span], back_one.at[span], p1s.at[c], p1r.at[c], behind(1))

    def one_stat():
        return remote(stat_one, bstat_one, t1s, t1r, behind(1))

    def far_part(j):
        return remote(part_far.at[j - 2], back_far.at[j - 2], pfs.at[j - 2], pfr.at[j - 2], behind(j))

    def far_stat(j):
        return remote(stat_far.at[j - 2], bstat_far.at[j - 2], tfs.at[j - 2], tfr.at[j - 2], behind(j))

    def w_half(r, which):
        return wbuf.at[r - 1, pl.ds(pl.multiple_of(which * half, half), half)]

    def w_near(i):
        return remote(
            w_own.at[pl.ds(pl.multiple_of(parity * half, half), half)],
            w_half(2 * i + 1, parity),
            ws.at[i],
            wr.at[i],
            (right, left)[i],
        )

    def w_onward(i):
        span = pl.ds(pl.multiple_of(parity * half + i * (half // 2), half // 2), half // 2)
        return remote(wbuf.at[2 * i, span], wbuf.at[1, span], us.at[i], ur.at[i], (right, left)[i])

    def w_pass(r, which):
        return remote(w_half(r, which), w_half(r, which), fs.at[r - 1], fr.at[r - 1], partner)

    def o_copy(r, c):
        s = lax.rem(t + r, n_tp)
        span = span_of(c)
        return remote(
            obuf.at[span, pl.ds(pl.multiple_of(s * share, share), share)],
            rbuf.at[r - 1, span],
            os_.at[r - 1, c],
            or_.at[r - 1, c],
            peers[r - 1],
        )

    def s_copy(r):
        return remote(srow, sbuf.at[r - 1], ss.at[r - 1], sr.at[r - 1], peers[r - 1])

    for j in range(1, pages):
        len_copy(j).start()
    for c in range(chunks):
        for i in range(2):
            x_near(i, c).start()

    per = 256 // draft
    wide = per * draft

    def ancestors(g):
        line = jnp.concatenate(
            [
                jnp.where(
                    parents[g * per + b : g * per + b + 1, :] < 0,
                    -1,
                    parents[g * per + b : g * per + b + 1, :] + b * draft,
                )
                for b in range(per)
            ],
            axis=1,
        )
        low = iota((wide, wide), 0)
        high = iota((wide, wide), 1)
        up = jnp.where((low == line) | (low == high), 1.0, 0.0)
        steps = max(1, (draft - 1).bit_length())
        for _ in range(steps):
            last = up.astype(BF)
            up = jnp.minimum(dot(last, last), 1.0)
        down = jnp.swapaxes(up, 0, 1)
        depth = jnp.sum(up, axis=0, keepdims=True) - 1.0
        hit = low == -1
        for b in range(per):
            hit = hit | (low == accept[g * per + b] + b * draft)
        chosen = jnp.sum(jnp.where(hit, down, 0.0), axis=0, keepdims=True)
        level = iota((draft, wide), 0).astype(F32)
        select[g] = jnp.where(level == depth, chosen, 0.0).astype(BF)
        for b in range(per):
            span = slice(b * draft, (b + 1) * draft)
            reach[g * per + b] = down[span, span]

    def x_arrive(c):
        for i in range(2):
            x_near(i, c).wait_recv()
            x_onward(i, c).start()

    groups = requests // per
    ancestors(0)
    for c in range(chunks // 2):
        x_arrive(c)
    for g in range(1, groups):
        ancestors(g)
    for c in range(chunks // 2, chunks):
        x_arrive(c)

    def columns_of(s):
        return pl.ds(pl.multiple_of(s * share, share), share)

    def put_x(c, s, value):
        x_v[2 * c : 2 * c + 2, :, columns_of(s)] = value.reshape(2, draft, share)

    loads[0].wait()
    for c in range(chunks):
        span = span_of(c)
        put_x(c, t, hidden[span])
        for r in (1, 3):
            put_x(c, lax.rem(t - r + n_tp, n_tp), xbuf[r - 1, span])
        for i in range(2):
            x_onward(i, c).wait_recv()
        put_x(c, lax.rem(t - 2 + n_tp, n_tp), xbuf[1, span])
        x = x_v[2 * c : 2 * c + 2].reshape(rows, full)
        both = (dot(x, weights[0]) * 0.125).astype(BF)
        for i in range(rows // draft):
            q[c * rows // draft + i] = both[i * draft : (i + 1) * draft]
        one_q(c).start()
        k[2 * c : 2 * c + 2] = dot(x, weights[1]).astype(BF).reshape(2, draft, width)
        v[2 * c : 2 * c + 2] = dot(x, weights[2]).astype(BF).reshape(2, draft, width)

    def long_pair(length):
        first = jnp.int32(requests)
        second = jnp.int32(0)
        for m in range(requests):
            is_long = length(m) > 2 * page_len
            first = jnp.where(is_long, jnp.minimum(first, m), first)
            second = jnp.where(is_long, jnp.maximum(second, m), second)
        return jnp.minimum(first, requests - 1), second

    mine = long_pair(lambda m: own_len[m])
    shorts = requests - longs
    short = [jnp.where(own_len[m] <= 2 * page_len, 1, 0) for m in range(requests)]
    before = [jnp.int32(0)]
    for m in range(requests - 1):
        before.append(before[m] + short[m])
    work = []
    for i in range(shorts):
        found = jnp.int32(0)
        for m in range(requests):
            found = jnp.where((short[m] == 1) & (before[m] == i), m, found)
        work.append(found)
    work += [mine[0], mine[1]]
    place_of = [jnp.where(short[m] == 1, before[m], shorts + m - before[m]) for m in range(requests)]
    for i in range(longs):
        qlong[i] = q[mine[i]]
    for j in range(pages - 1, 1, -1):
        far_q(j).start()
    for i in range(2):
        w_near(i).start()

    for j in range(1, pages):
        len_copy(j).wait_recv()
    lens_in = pltpu.make_async_copy(lbuf, far_len, load_sem.at[4])
    lens_in.start()

    mask = jnp.where(
        iota((4 * draft, width), 0) // draft == iota((4 * draft, width), 1) // HD, 1.0, 0.0
    ).astype(BF)

    loads[1].wait()
    lens_in.wait()

    def page_of(slot):
        return pages_v[slot].reshape(2 * page_len, width)

    stats = jnp.zeros((4 * draft, 128), F32)
    for c in range(chunks):
        one_q(c).wait_recv()
        for i in range(2):
            r = 2 * c + i
            count = far_len[0, 0, r] - page_len
            queries = diagonal(q_one[r], mask)
            part, top, total = page_part(queries, page_of(page_table[1, r]), count, draft)
            part_one[r] = part.astype(BF)
            stats = place(place(stats, top, 2 * r), total, 2 * r + 1)
        one_part(c).start()
    turned = jnp.swapaxes(stats, 0, 1)
    for r in range(requests):
        stat_one[r] = turned[2 * r : 2 * r + 2]
    one_stat().start()

    def far_pages(j):
        pair = long_pair(lambda m: far_len[j - 1, 0, m])
        far_q(j).wait_recv()
        stats = jnp.zeros((4 * draft, 128), F32)
        for i in range(longs):
            slot = page_table[j, 0]
            count = far_len[j - 1, 0, 0]
            for m in range(1, requests):
                slot = jnp.where(pair[i] == m, page_table[j, m], slot)
                count = jnp.where(pair[i] == m, far_len[j - 1, 0, m], count)
            count = count - j * page_len
            queries = diagonal(q_far[j - 2, i], mask)
            part, top, total = page_part(queries, page_of(slot), count, draft)
            part_far[j - 2, i * draft : (i + 1) * draft] = part.astype(BF)
            stats = place(place(stats, top, 2 * i), total, 2 * i + 1)
        stat_far[j - 2] = jnp.swapaxes(stats, 0, 1)[0:8]
        far_part(j).start()
        far_stat(j).start()

    def own(p):
        r = work[p]
        queries = diagonal(q[r], mask)
        part, top, total = page_part(queries, page_of(page_table[0, r]), own_len[r], draft)
        allowed = jnp.concatenate([reach[r]] * 4, axis=0) > 0.5
        scores = dot_t(queries, k[r])
        tree_top = jnp.max(jnp.where(allowed, scores, NEG), axis=1, keepdims=True)
        best = jnp.maximum(top, tree_top)
        weight = jnp.where(allowed, jnp.exp(scores - best), 0.0).astype(BF)
        scale = jnp.exp(top - best)
        total = total * scale + jnp.sum(weight.astype(F32), axis=1, keepdims=True)
        tree = fold(dot(weight, v[r]), draft)
        acc[p] = part * spread(scale, draft) + tree
        own_stat[p] = place(place(jnp.zeros((4 * draft, 128), F32), best, 0), total, 1)

    def long_parts():
        for j in range(pages - 1, 1, -1):
            far_stat(j).wait_recv()
            far_part(j).wait_recv()
        far_columns = jnp.swapaxes(
            jnp.concatenate(
                [bstat_far[j - 2] for j in range(2, pages)]
                + [jnp.zeros((128 - 8 * (pages - 2), 4 * draft), F32)],
                axis=0,
            ),
            0,
            1,
        )
        found = []
        for i in range(longs):
            at = [8 * (j - 2) + 2 * i for j in range(2, pages)]
            tops = [far_columns[:, a : a + 1] for a in at]
            sums = [far_columns[:, a + 1 : a + 2] for a in at]
            best = functools.reduce(jnp.maximum, tops)
            total = jnp.zeros_like(best)
            whole = jnp.zeros((draft, width), F32)
            for j in range(2, pages):
                scale = jnp.exp(tops[j - 2] - best)
                total = total + scale * sums[j - 2]
                part = back_far[j - 2, i * draft : (i + 1) * draft].astype(F32)
                whole = whole + spread(scale, draft) * part
            found.append((whole, best, total))
        return found

    def combine(c, one_columns, found=None):
        for i in range(2):
            p = 2 * c + i
            stat = own_stat[p]
            top_o = stat[:, 0:1]
            total_o = stat[:, 1:2]
            top_1 = one_columns[:, 2 * p : 2 * p + 1]
            total_1 = one_columns[:, 2 * p + 1 : 2 * p + 2]
            best = jnp.maximum(top_o, top_1)
            if found is not None:
                acc_l, top_l, total_l = found[i]
                best = jnp.maximum(best, top_l)
            s_o = jnp.exp(top_o - best)
            s_1 = jnp.exp(top_1 - best)
            whole = s_o * total_o + s_1 * total_1
            if found is not None:
                s_l = jnp.exp(top_l - best)
                whole = whole + s_l * total_l
            whole = 1.0 / whole
            y = acc[p] * spread(s_o * whole, draft)
            y = y + back_one[work[p]].astype(F32) * spread(s_1 * whole, draft)
            if found is not None:
                y = y + acc_l * spread(s_l * whole, draft)
            att[p * draft : (p + 1) * draft] = y.astype(BF)
        for i in range(2):
            a_near(i, c).start()

    def a_arrive(c):
        for i in range(2):
            a_near(i, c).wait_recv()
            a_onward(i, c).start()

    for i in range(2):
        w_near(i).wait_recv()
        w_onward(i).start()
    for p in range(4):
        own(p)
    one_stat().wait_recv()
    for c in range(chunks):
        one_part(c).wait_recv()
    one_columns = jnp.swapaxes(
        jnp.concatenate(
            [bstat_one[work[p]] for p in range(requests)] + [jnp.zeros((128 - 16, 4 * draft), F32)],
            axis=0,
        ),
        0,
        1,
    )
    combine(0, one_columns)
    combine(1, one_columns)

    for i in range(2):
        w_onward(i).wait_recv()
    for r in range(1, n_tp):
        w_pass(r, parity).start()
    for j in range(pages - 1, 1, -1):
        far_pages(j)
        if j == pages - 2:
            a_arrive(0)
        if j == pages - 3:
            a_arrive(1)
    own(4)
    own(5)
    combine(2, one_columns)
    own(6)
    own(7)

    for r in range(1, n_tp):
        w_pass(r, 1 - parity).wait_recv()
    loads[2].wait()
    loads[3].wait()
    order = [1, 3, 2]
    mine_cols = columns_of(t)
    for c in range(chunks):
        span = span_of(c)
        if c == 1:
            a_arrive(2)
        if c == 2:
            combine(3, one_columns, long_parts())
        if c == 3:
            a_arrive(3)
        branch = dot(att[span], w_own[...])
        for r in (1, 3):
            branch = branch + dot(abuf[r - 1, span], wbuf[r - 1])
        for i in range(2):
            a_onward(i, c).wait_recv()
        branch = branch + dot(abuf[1, span], wbuf[1])
        x = jnp.concatenate([x_v[work[2 * c]], x_v[work[2 * c + 1]]], axis=0)
        z = x.astype(F32) + branch
        center = jnp.sum(z, axis=1, keepdims=True) / full
        var = jnp.sum(z * z, axis=1, keepdims=True) / full - center * center
        normed = ((z - center) * lax.rsqrt(var + EPS) * gain1[...]).astype(BF)
        normed_v[...] = normed
        share_v[span] = normed_v[:, mine_cols]
        pre = dot(normed, w_up[...])
        inner = (0.5 * pre * (1.0 + lax.erf(pre * 0.7071067811865476))).astype(BF)
        obuf[span] = dot(inner, w_down[...]).astype(BF)
        for r in order:
            o_copy(r, c).start()

    for r in range(requests):
        b = r % per
        pick = select[r // per][:, b * draft : (b + 1) * draft]
        kept[r, :, 0:width] = dot(pick, k[r]).astype(BF)
        kept[r, :, width : 2 * width] = dot(pick, v[r]).astype(BF)

    lane = iota((rows, 128), 1)
    stats = jnp.zeros((rows, 128), F32)
    for c in range(chunks):
        span = span_of(c)
        y = share_v[span].astype(F32) + obuf[span, mine_cols].astype(F32)
        for r in range(1, n_tp):
            o_copy(r, c).wait_recv()
            y = y + rbuf[r - 1, span].astype(F32)
        second_v[span] = y
        stats = jnp.where(lane == 2 * c, jnp.sum(y, axis=1, keepdims=True), stats)
        stats = jnp.where(lane == 2 * c + 1, jnp.sum(y * y, axis=1, keepdims=True), stats)
    total = jnp.swapaxes(stats, 0, 1)[0:8]
    srow[...] = total
    for r in order:
        s_copy(r).start()
    for r in range(1, n_tp):
        s_copy(r).wait_recv()
        total = total + sbuf[r - 1]
    columns = jnp.swapaxes(
        jnp.concatenate([total, jnp.zeros((128 - 8, rows), F32)], axis=0), 0, 1
    )
    for c in range(chunks):
        span = span_of(c)
        center = columns[:, 2 * c : 2 * c + 1] / full
        var = columns[:, 2 * c + 1 : 2 * c + 2] / full - center * center
        y = (second_v[span] - center) * lax.rsqrt(var + EPS) * gain2[:, mine_cols]
        done[2 * c : 2 * c + 2] = y.astype(BF).reshape(2, draft, share)
    for r in range(requests):
        out[r * draft : (r + 1) * draft] = done[place_of[r]]

    for j in range(1, pages):
        len_copy(j).wait_send()
    for j in range(2, pages):
        far_q(j).wait_send()
        far_part(j).wait_send()
        far_stat(j).wait_send()
    one_stat().wait_send()
    for c in range(chunks):
        one_q(c).wait_send()
        one_part(c).wait_send()
        for i in range(2):
            x_near(i, c).wait_send()
            x_onward(i, c).wait_send()
            a_near(i, c).wait_send()
            a_onward(i, c).wait_send()
    for i in range(2):
        w_near(i).wait_send()
        w_onward(i).wait_send()
    for r in range(1, n_tp):
        w_pass(r, parity).wait_send()
        s_copy(r).wait_send()
        for c in range(chunks):
            o_copy(r, c).wait_send()


def layer(
    sizes, hidden, w_own, gain1, gain2, parents, accept, page_table, own_len, w_qkv, w_up, w_down, pool
):
    n_req, n_tp, pages, chunks = sizes
    tokens, share = hidden.shape
    requests, draft = parents.shape
    full = share * n_tp
    rows = tokens // chunks
    far = pages - 2
    others = n_tp - 1
    vm = pl.BlockSpec(memory_space=pltpu.VMEM)
    sm = pl.BlockSpec(memory_space=pltpu.SMEM)
    hbm = pl.BlockSpec(memory_space=pl.ANY)
    sds = jax.ShapeDtypeStruct
    dma = pltpu.SemaphoreType.DMA
    vmem = pltpu.VMEM
    pairs = [dma(s) for s in [(2, chunks), (2, chunks), (pages - 1,), (chunks,), (far,), (chunks,)] for _ in range(2)]
    pairs += [dma, dma]
    pairs += [
        dma(s)
        for s in [(far,), (far,), (2,), (2,), (others,), (2, chunks), (2, chunks), (others, chunks), (others,)]
        for _ in range(2)
    ]
    return pl.pallas_call(
        functools.partial(layer_kernel, sizes),
        out_shape=(
            sds((tokens, share), BF),
            sds((requests, draft, 2 * share), BF),
        ),
        in_specs=[vm, vm, vm, vm, vm, sm, sm, sm, hbm, hbm, hbm, hbm],
        out_specs=(vm,) * 2,
        scratch_shapes=[
            vmem(w_qkv.shape, BF),
            vmem(w_up.shape, BF),
            vmem(w_down.shape, BF),
            vmem(pool.shape, BF),
            dma((5,)),
            vmem((requests, draft, full), BF),
            vmem((requests, draft, share), BF),
            vmem((requests, draft, share), BF),
            vmem((requests, draft, share), BF),
            vmem((requests, draft, draft), F32),
            vmem((requests * draft // 256, draft, 256), BF),
            vmem((1, 128), jnp.int32),
            vmem((pages - 1, 1, 128), jnp.int32),
            pltpu.SMEM((pages - 1, 1, 128), jnp.int32),
            vmem((others, tokens, share), BF),
            vmem((2, draft, share), BF),
            vmem((requests, draft, share), BF),
            vmem((far, 2, draft, share), BF),
            vmem((requests, draft, share), BF),
            vmem((requests, 2, 4 * draft), F32),
            vmem((far, 2 * draft, share), BF),
            vmem((far, 8, 4 * draft), F32),
            vmem((requests, draft, share), BF),
            vmem((requests, 2, 4 * draft), F32),
            vmem((far, 2 * draft, share), BF),
            vmem((far, 8, 4 * draft), F32),
            vmem((requests, draft, share), F32),
            vmem((requests, 4 * draft, 128), F32),
            vmem((others,) + w_own.shape, BF),
            vmem((tokens, share), BF),
            vmem((others, tokens, share), BF),
            vmem((rows, full), BF),
            vmem((tokens, share), BF),
            vmem((tokens, full), BF),
            vmem((others, tokens, share), BF),
            vmem((tokens, share), F32),
            vmem((requests, draft, share), BF),
            vmem((8, rows), F32),
            vmem((others, 8, rows), F32),
        ]
        + pairs,
        compiler_params=pltpu.CompilerParams(
            collective_id=0, has_side_effects=True, vmem_limit_bytes=VMEM_BYTES
        ),
        name="layer",
    )(
        hidden,
        w_own,
        gain1.reshape(1, -1),
        gain2.reshape(1, -1),
        parents,
        accept,
        page_table,
        own_len,
        w_qkv,
        w_up,
        w_down,
        pool,
    )


def shards(
    sizes,
    hidden_in,
    w_qkv,
    w_out,
    first_gain,
    w_up,
    w_down,
    second_gain,
    cache_pool,
    page_table,
    cache_len,
    tree_parent,
    accept_node,
):
    layer_out, kept = layer(
        sizes,
        hidden_in,
        w_out,
        first_gain,
        second_gain,
        tree_parent,
        accept_node,
        page_table,
        cache_len,
        jnp.transpose(w_qkv, (1, 0, 2)),
        w_up,
        w_down,
        cache_pool,
    )
    requests, draft = tree_parent.shape
    return layer_out, kept.reshape(requests, draft, 2, -1)


def solution(mesh):
    placed = (
        P("req", "tp"),
        P(None, None, "tp"),
        P("tp", None),
        P(),
        P(None, "tp"),
        P("tp", None),
        P(),
        P("req", None, None, "tp"),
        P("req", None),
        P("req"),
        P("req", None),
        P("req"),
    )
    sizes = (mesh.shape["req"], mesh.shape["tp"], 8, 4)
    return jax.shard_map(
        functools.partial(shards, sizes),
        mesh=mesh,
        in_specs=placed,
        out_specs=(P("req", "tp"), P("req", None, None, "tp")),
        check_vma=False,
    )
```

```python
import functools

import jax
import jax.numpy as jnp
from jax import lax
from jax.experimental import pallas as pl
from jax.experimental.pallas import tpu as pltpu
from jax.sharding import PartitionSpec as P

HD = 64
NEG = -1e30
EPS = 1e-05
BF = jnp.bfloat16
F32 = jnp.float32
MESH = pl.DeviceIdType.MESH
VMEM_BYTES = 60 * 2**20


def dot(a, b):
    return jnp.dot(a, b, preferred_element_type=F32)


def dot_t(a, b):
    return lax.dot_general(a, b, (((1,), (1,)), ((), ())), preferred_element_type=F32)


def iota(shape, dim):
    return lax.broadcasted_iota(jnp.int32, shape, dim)


def remote(src, dst, ssem, rsem, dev):
    return pltpu.make_async_remote_copy(
        src_ref=src, dst_ref=dst, send_sem=ssem, recv_sem=rsem, device_id=dev, device_id_type=MESH
    )


def greet(devices):
    barrier = pltpu.get_barrier_semaphore()
    for dev in devices:
        pl.semaphore_signal(barrier, inc=1, device_id=dev, device_id_type=MESH)
    pl.semaphore_wait(barrier, len(devices))


def diagonal(rows64, mask):
    return jnp.concatenate([rows64] * 4, axis=0) * mask


def fold(wide, draft):
    lane = iota((draft, wide.shape[1]), 1)
    out = wide[0:draft]
    for h in range(1, wide.shape[1] // HD):
        out = jnp.where(lane >= h * HD, wide[h * draft : (h + 1) * draft], out)
    return out


def page_part(queries, page, count, draft):
    n = page.shape[0] // 2
    row = iota((2 * n, 2 * n), 0)
    wanted = jnp.where(row < n, 2 * row, 2 * (row - n) + 1)
    pick = jnp.where(iota((2 * n, 2 * n), 1) == wanted, 1.0, 0.0).astype(BF)
    both = dot(pick, page).astype(BF)
    scores = dot_t(queries, both[:n])
    valid = iota(scores.shape, 1) < count
    top = jnp.max(jnp.where(valid, scores, NEG), axis=1, keepdims=True)
    weights = jnp.where(valid, jnp.exp(scores - top), 0.0).astype(BF)
    total = jnp.sum(weights.astype(F32), axis=1, keepdims=True)
    return fold(dot(weights, both[n:]), draft), top, total


def spread(column, draft):
    lane = iota((draft, 128), 1)
    tiles = []
    for i in range(2):
        a = jnp.broadcast_to(column[2 * i * draft : (2 * i + 1) * draft], (draft, 128))
        b = jnp.broadcast_to(column[(2 * i + 1) * draft : (2 * i + 2) * draft], (draft, 128))
        tiles.append(jnp.where(lane < HD, a, b))
    return jnp.concatenate(tiles, axis=1)


def place(stats, column, at):
    lane = iota(stats.shape, 1)
    return jnp.where(lane == at, column, stats)


def layer_kernel(
    sizes,
    hidden,
    w_own,
    gain1,
    gain2,
    parents,
    accept,
    page_table,
    own_len,
    qkv_hbm,
    up_hbm,
    down_hbm,
    pool,
    out,
    kept,
    weights,
    w_up,
    w_down,
    pages_v,
    load_sem,
    x_v,
    q,
    k,
    v,
    reach,
    select,
    lens_row,
    lbuf,
    far_len,
    xbuf,
    qlong,
    q_one,
    q_far,
    part_one,
    stat_one,
    part_far,
    stat_far,
    back_one,
    bstat_one,
    back_far,
    bstat_far,
    acc,
    own_stat,
    wbuf,
    att,
    abuf,
    normed_v,
    share_v,
    obuf,
    rbuf,
    second_v,
    done,
    srow,
    sbuf,
    xs,
    xr,
    vs,
    vr,
    ls,
    lr,
    q1s,
    q1r,
    qfs,
    qfr,
    p1s,
    p1r,
    t1s,
    t1r,
    pfs,
    pfr,
    tfs,
    tfr,
    ws,
    wr,
    us,
    ur,
    fs,
    fr,
    as_,
    ar,
    bs,
    br,
    os_,
    or_,
    ss,
    sr,
):
    n_req, n_tp, pages, chunks = sizes
    e = lax.axis_index("req")
    t = lax.axis_index("tp")
    tokens, share = hidden.shape
    requests, draft = parents.shape
    rows = tokens // chunks
    step = rows // 2
    width = share
    full = share * n_tp
    page_len = pages_v.shape[1]
    longs = (requests + 3) // 4
    half = w_own.shape[0] // 2
    parity = lax.rem(e, 2)
    partner = (e + 1 - 2 * parity, t)
    peers = [(e, lax.rem(t + r, n_tp)) for r in range(1, n_tp)]
    right, left = peers[0], peers[2]

    def ahead(j):
        return (lax.rem(e + j, n_req), t)

    def behind(j):
        return (lax.rem(e - j + n_req, n_req), t)

    loads = [
        pltpu.make_async_copy(a, b, load_sem.at[i])
        for i, (a, b) in enumerate(
            [(qkv_hbm, weights), (pool, pages_v), (up_hbm, w_up), (down_hbm, w_down)]
        )
    ]
    for load in loads:
        load.start()

    lane_row = iota((1, 128), 1)
    line = jnp.zeros((1, 128), jnp.int32)
    for m in range(requests):
        line = jnp.where(lane_row == m, own_len[m], line)
    lens_row[...] = line

    greet(peers + [ahead(j) for j in range(1, pages)] + [behind(j) for j in range(1, pages)])

    def span_of(c):
        return pl.ds(c * rows, rows)

    def part_of(c, i):
        return pl.ds(c * rows + i * step, step)

    def len_copy(j):
        return remote(lens_row, lbuf.at[j - 1], ls.at[j - 1], lr.at[j - 1], ahead(j))

    def near(source, buf, send, recv, i, c):
        span = span_of(c)
        return remote(
            source.at[span], buf.at[2 * i, span], send.at[i, c], recv.at[i, c], (right, left)[i]
        )

    def onward(buf, send, recv, i, c):
        span = part_of(c, i)
        return remote(
            buf.at[2 * i, span], buf.at[1, span], send.at[i, c], recv.at[i, c], (right, left)[i]
        )

    def x_near(i, c):
        return near(hidden, xbuf, xs, xr, i, c)

    def x_onward(i, c):
        return onward(xbuf, vs, vr, i, c)

    def a_near(i, c):
        return near(att, abuf, as_, ar, i, c)

    def a_onward(i, c):
        return onward(abuf, bs, br, i, c)

    def far_q(j):
        return remote(qlong, q_far.at[j - 2], qfs.at[j - 2], qfr.at[j - 2], ahead(j))

    def one_q(c):
        span = pl.ds(2 * c, 2)
        return remote(q.at[span], q_one.at[span], q1s.at[c], q1r.at[c], ahead(1))

    def one_part(c):
        span = pl.ds(2 * c, 2)
        return remote(part_one.at[span], back_one.at[span], p1s.at[c], p1r.at[c], behind(1))

    def one_stat():
        return remote(stat_one, bstat_one, t1s, t1r, behind(1))

    def far_part(j):
        return remote(part_far.at[j - 2], back_far.at[j - 2], pfs.at[j - 2], pfr.at[j - 2], behind(j))

    def far_stat(j):
        return remote(stat_far.at[j - 2], bstat_far.at[j - 2], tfs.at[j - 2], tfr.at[j - 2], behind(j))

    def w_half(r, which):
        return wbuf.at[r - 1, pl.ds(pl.multiple_of(which * half, half), half)]

    def w_near(i):
        return remote(
            w_own.at[pl.ds(pl.multiple_of(parity * half, half), half)],
            w_half(2 * i + 1, parity),
            ws.at[i],
            wr.at[i],
            (right, left)[i],
        )

    def w_onward(i):
        span = pl.ds(pl.multiple_of(parity * half + i * (half // 2), half // 2), half // 2)
        return remote(wbuf.at[2 * i, span], wbuf.at[1, span], us.at[i], ur.at[i], (right, left)[i])

    def w_pass(r, which):
        return remote(w_half(r, which), w_half(r, which), fs.at[r - 1], fr.at[r - 1], partner)

    def o_copy(r, c):
        s = lax.rem(t + r, n_tp)
        span = span_of(c)
        return remote(
            obuf.at[span, pl.ds(pl.multiple_of(s * share, share), share)],
            rbuf.at[r - 1, span],
            os_.at[r - 1, c],
            or_.at[r - 1, c],
            peers[r - 1],
        )

    def s_copy(r):
        return remote(srow, sbuf.at[r - 1], ss.at[r - 1], sr.at[r - 1], peers[r - 1])

    for j in range(1, pages):
        len_copy(j).start()
    for c in range(chunks):
        for i in range(2):
            x_near(i, c).start()

    per = 256 // draft
    wide = per * draft

    def ancestors(g):
        line = jnp.concatenate(
            [
                jnp.where(
                    parents[g * per + b : g * per + b + 1, :] < 0,
                    -1,
                    parents[g * per + b : g * per + b + 1, :] + b * draft,
                )
                for b in range(per)
            ],
            axis=1,
        )
        low = iota((wide, wide), 0)
        high = iota((wide, wide), 1)
        up = jnp.where((low == line) | (low == high), 1.0, 0.0)
        steps = max(1, (draft - 1).bit_length())
        for _ in range(steps):
            last = up.astype(BF)
            up = jnp.minimum(dot(last, last), 1.0)
        down = jnp.swapaxes(up, 0, 1)
        depth = jnp.sum(up, axis=0, keepdims=True) - 1.0
        hit = low == -1
        for b in range(per):
            hit = hit | (low == accept[g * per + b] + b * draft)
        chosen = jnp.sum(jnp.where(hit, down, 0.0), axis=0, keepdims=True)
        level = iota((draft, wide), 0).astype(F32)
        select[g] = jnp.where(level == depth, chosen, 0.0).astype(BF)
        for b in range(per):
            span = slice(b * draft, (b + 1) * draft)
            reach[g * per + b] = down[span, span]

    def x_arrive(c):
        for i in range(2):
            x_near(i, c).wait_recv()
            x_onward(i, c).start()

    groups = requests // per
    ancestors(0)
    for c in range(chunks // 2):
        x_arrive(c)
    for g in range(1, groups):
        ancestors(g)
    for c in range(chunks // 2, chunks):
        x_arrive(c)

    def columns_of(s):
        return pl.ds(pl.multiple_of(s * share, share), share)

    def put_x(c, s, value):
        x_v[2 * c : 2 * c + 2, :, columns_of(s)] = value.reshape(2, draft, share)

    loads[0].wait()
    for c in range(chunks):
        span = span_of(c)
        put_x(c, t, hidden[span])
        for r in (1, 3):
            put_x(c, lax.rem(t - r + n_tp, n_tp), xbuf[r - 1, span])
        for i in range(2):
            x_onward(i, c).wait_recv()
        put_x(c, lax.rem(t - 2 + n_tp, n_tp), xbuf[1, span])
        x = x_v[2 * c : 2 * c + 2].reshape(rows, full)
        both = (dot(x, weights[0]) * 0.125).astype(BF)
        for i in range(rows // draft):
            q[c * rows // draft + i] = both[i * draft : (i + 1) * draft]
        one_q(c).start()
        k[2 * c : 2 * c + 2] = dot(x, weights[1]).astype(BF).reshape(2, draft, width)
        v[2 * c : 2 * c + 2] = dot(x, weights[2]).astype(BF).reshape(2, draft, width)

    def long_pair(length):
        first = jnp.int32(requests)
        second = jnp.int32(0)
        for m in range(requests):
            is_long = length(m) > 2 * page_len
            first = jnp.where(is_long, jnp.minimum(first, m), first)
            second = jnp.where(is_long, jnp.maximum(second, m), second)
        return jnp.minimum(first, requests - 1), second

    mine = long_pair(lambda m: own_len[m])
    shorts = requests - longs
    short = [jnp.where(own_len[m] <= 2 * page_len, 1, 0) for m in range(requests)]
    before = [jnp.int32(0)]
    for m in range(requests - 1):
        before.append(before[m] + short[m])
    work = []
    for i in range(shorts):
        found = jnp.int32(0)
        for m in range(requests):
            found = jnp.where((short[m] == 1) & (before[m] == i), m, found)
        work.append(found)
    work += [mine[0], mine[1]]
    place_of = [jnp.where(short[m] == 1, before[m], shorts + m - before[m]) for m in range(requests)]
    for i in range(longs):
        qlong[i] = q[mine[i]]
    for j in range(pages - 1, 1, -1):
        far_q(j).start()
    for i in range(2):
        w_near(i).start()

    for j in range(1, pages):
        len_copy(j).wait_recv()
    lens_in = pltpu.make_async_copy(lbuf, far_len, load_sem.at[4])
    lens_in.start()

    mask = jnp.where(
        iota((4 * draft, width), 0) // draft == iota((4 * draft, width), 1) // HD, 1.0, 0.0
    ).astype(BF)

    loads[1].wait()
    lens_in.wait()

    def page_of(slot):
        return pages_v[slot].reshape(2 * page_len, width)

    stats = jnp.zeros((4 * draft, 128), F32)
    for c in range(chunks):
        one_q(c).wait_recv()
        for i in range(2):
            r = 2 * c + i
            count = far_len[0, 0, r] - page_len
            queries = diagonal(q_one[r], mask)
            part, top, total = page_part(queries, page_of(page_table[1, r]), count, draft)
            part_one[r] = part.astype(BF)
            stats = place(place(stats, top, 2 * r), total, 2 * r + 1)
        one_part(c).start()
    turned = jnp.swapaxes(stats, 0, 1)
    for r in range(requests):
        stat_one[r] = turned[2 * r : 2 * r + 2]
    one_stat().start()

    def far_pages(j):
        pair = long_pair(lambda m: far_len[j - 1, 0, m])
        far_q(j).wait_recv()
        stats = jnp.zeros((4 * draft, 128), F32)
        for i in range(longs):
            slot = page_table[j, 0]
            count = far_len[j - 1, 0, 0]
            for m in range(1, requests):
                slot = jnp.where(pair[i] == m, page_table[j, m], slot)
                count = jnp.where(pair[i] == m, far_len[j - 1, 0, m], count)
            count = count - j * page_len
            queries = diagonal(q_far[j - 2, i], mask)
            part, top, total = page_part(queries, page_of(slot), count, draft)
            part_far[j - 2, i * draft : (i + 1) * draft] = part.astype(BF)
            stats = place(place(stats, top, 2 * i), total, 2 * i + 1)
        stat_far[j - 2] = jnp.swapaxes(stats, 0, 1)[0:8]
        far_part(j).start()
        far_stat(j).start()

    def own(p):
        r = work[p]
        queries = diagonal(q[r], mask)
        part, top, total = page_part(queries, page_of(page_table[0, r]), own_len[r], draft)
        allowed = jnp.concatenate([reach[r]] * 4, axis=0) > 0.5
        scores = dot_t(queries, k[r])
        tree_top = jnp.max(jnp.where(allowed, scores, NEG), axis=1, keepdims=True)
        best = jnp.maximum(top, tree_top)
        weight = jnp.where(allowed, jnp.exp(scores - best), 0.0).astype(BF)
        scale = jnp.exp(top - best)
        total = total * scale + jnp.sum(weight.astype(F32), axis=1, keepdims=True)
        tree = fold(dot(weight, v[r]), draft)
        acc[p] = part * spread(scale, draft) + tree
        own_stat[p] = place(place(jnp.zeros((4 * draft, 128), F32), best, 0), total, 1)

    def long_parts():
        for j in range(pages - 1, 1, -1):
            far_stat(j).wait_recv()
            far_part(j).wait_recv()
        far_columns = jnp.swapaxes(
            jnp.concatenate(
                [bstat_far[j - 2] for j in range(2, pages)]
                + [jnp.zeros((128 - 8 * (pages - 2), 4 * draft), F32)],
                axis=0,
            ),
            0,
            1,
        )
        found = []
        for i in range(longs):
            at = [8 * (j - 2) + 2 * i for j in range(2, pages)]
            tops = [far_columns[:, a : a + 1] for a in at]
            sums = [far_columns[:, a + 1 : a + 2] for a in at]
            best = functools.reduce(jnp.maximum, tops)
            total = jnp.zeros_like(best)
            whole = jnp.zeros((draft, width), F32)
            for j in range(2, pages):
                scale = jnp.exp(tops[j - 2] - best)
                total = total + scale * sums[j - 2]
                part = back_far[j - 2, i * draft : (i + 1) * draft].astype(F32)
                whole = whole + spread(scale, draft) * part
            found.append((whole, best, total))
        return found

    def combine(c, one_columns, found=None):
        for i in range(2):
            p = 2 * c + i
            stat = own_stat[p]
            top_o = stat[:, 0:1]
            total_o = stat[:, 1:2]
            top_1 = one_columns[:, 2 * p : 2 * p + 1]
            total_1 = one_columns[:, 2 * p + 1 : 2 * p + 2]
            best = jnp.maximum(top_o, top_1)
            if found is not None:
                acc_l, top_l, total_l = found[i]
                best = jnp.maximum(best, top_l)
            s_o = jnp.exp(top_o - best)
            s_1 = jnp.exp(top_1 - best)
            whole = s_o * total_o + s_1 * total_1
            if found is not None:
                s_l = jnp.exp(top_l - best)
                whole = whole + s_l * total_l
            whole = 1.0 / whole
            y = acc[p] * spread(s_o * whole, draft)
            y = y + back_one[work[p]].astype(F32) * spread(s_1 * whole, draft)
            if found is not None:
                y = y + acc_l * spread(s_l * whole, draft)
            att[p * draft : (p + 1) * draft] = y.astype(BF)
        for i in range(2):
            a_near(i, c).start()

    def a_arrive(c):
        for i in range(2):
            a_near(i, c).wait_recv()
            a_onward(i, c).start()

    for i in range(2):
        w_near(i).wait_recv()
        w_onward(i).start()
    for p in range(4):
        own(p)
    one_stat().wait_recv()
    for c in range(chunks):
        one_part(c).wait_recv()
    one_columns = jnp.swapaxes(
        jnp.concatenate(
            [bstat_one[work[p]] for p in range(requests)] + [jnp.zeros((128 - 16, 4 * draft), F32)],
            axis=0,
        ),
        0,
        1,
    )
    combine(0, one_columns)
    combine(1, one_columns)

    for i in range(2):
        w_onward(i).wait_recv()
    for r in range(1, n_tp):
        w_pass(r, parity).start()
    for j in range(pages - 1, 1, -1):
        far_pages(j)
        if j == pages - 2:
            a_arrive(0)
        if j == pages - 3:
            a_arrive(1)
    own(4)
    own(5)
    combine(2, one_columns)
    own(6)
    own(7)

    for r in range(1, n_tp):
        w_pass(r, 1 - parity).wait_recv()
    loads[2].wait()
    loads[3].wait()
    order = [1, 3, 2]
    mine_cols = columns_of(t)
    for c in range(chunks):
        span = span_of(c)
        if c == 1:
            a_arrive(2)
        if c == 2:
            combine(3, one_columns, long_parts())
        if c == 3:
            a_arrive(3)
        branch = dot(att[span], w_own[...])
        for r in (1, 3):
            branch = branch + dot(abuf[r - 1, span], wbuf[r - 1])
        for i in range(2):
            a_onward(i, c).wait_recv()
        branch = branch + dot(abuf[1, span], wbuf[1])
        x = jnp.concatenate([x_v[work[2 * c]], x_v[work[2 * c + 1]]], axis=0)
        z = x.astype(F32) + branch
        center = jnp.sum(z, axis=1, keepdims=True) / full
        var = jnp.sum(z * z, axis=1, keepdims=True) / full - center * center
        normed = ((z - center) * lax.rsqrt(var + EPS) * gain1[...]).astype(BF)
        normed_v[...] = normed
        share_v[span] = normed_v[:, mine_cols]
        pre = dot(normed, w_up[...])
        inner = (0.5 * pre * (1.0 + lax.erf(pre * 0.7071067811865476))).astype(BF)
        obuf[span] = dot(inner, w_down[...]).astype(BF)
        for r in order:
            o_copy(r, c).start()

    for r in range(requests):
        b = r % per
        pick = select[r // per][:, b * draft : (b + 1) * draft]
        kept[r, :, 0:width] = dot(pick, k[r]).astype(BF)
        kept[r, :, width : 2 * width] = dot(pick, v[r]).astype(BF)

    lane = iota((rows, 128), 1)
    stats = jnp.zeros((rows, 128), F32)
    for c in range(chunks):
        span = span_of(c)
        y = share_v[span].astype(F32) + obuf[span, mine_cols].astype(F32)
        for r in range(1, n_tp):
            o_copy(r, c).wait_recv()
            y = y + rbuf[r - 1, span].astype(F32)
        second_v[span] = y
        stats = jnp.where(lane == 2 * c, jnp.sum(y, axis=1, keepdims=True), stats)
        stats = jnp.where(lane == 2 * c + 1, jnp.sum(y * y, axis=1, keepdims=True), stats)
    total = jnp.swapaxes(stats, 0, 1)[0:8]
    srow[...] = total
    for r in order:
        s_copy(r).start()
    for r in range(1, n_tp):
        s_copy(r).wait_recv()
        total = total + sbuf[r - 1]
    columns = jnp.swapaxes(
        jnp.concatenate([total, jnp.zeros((128 - 8, rows), F32)], axis=0), 0, 1
    )
    for c in range(chunks):
        span = span_of(c)
        center = columns[:, 2 * c : 2 * c + 1] / full
        var = columns[:, 2 * c + 1 : 2 * c + 2] / full - center * center
        y = (second_v[span] - center) * lax.rsqrt(var + EPS) * gain2[:, mine_cols]
        done[2 * c : 2 * c + 2] = y.astype(BF).reshape(2, draft, share)
    for r in range(requests):
        out[r * draft : (r + 1) * draft] = done[place_of[r]]

    for j in range(1, pages):
        len_copy(j).wait_send()
    for j in range(2, pages):
        far_q(j).wait_send()
        far_part(j).wait_send()
        far_stat(j).wait_send()
    one_stat().wait_send()
    for c in range(chunks):
        one_q(c).wait_send()
        one_part(c).wait_send()
        for i in range(2):
            x_near(i, c).wait_send()
            x_onward(i, c).wait_send()
            a_near(i, c).wait_send()
            a_onward(i, c).wait_send()
    for i in range(2):
        w_near(i).wait_send()
        w_onward(i).wait_send()
    for r in range(1, n_tp):
        w_pass(r, parity).wait_send()
        s_copy(r).wait_send()
        for c in range(chunks):
            o_copy(r, c).wait_send()


def layer(
    sizes, hidden, w_own, gain1, gain2, parents, accept, page_table, own_len, w_qkv, w_up, w_down, pool
):
    n_req, n_tp, pages, chunks = sizes
    tokens, share = hidden.shape
    requests, draft = parents.shape
    full = share * n_tp
    rows = tokens // chunks
    far = pages - 2
    others = n_tp - 1
    vm = pl.BlockSpec(memory_space=pltpu.VMEM)
    sm = pl.BlockSpec(memory_space=pltpu.SMEM)
    hbm = pl.BlockSpec(memory_space=pl.ANY)
    sds = jax.ShapeDtypeStruct
    dma = pltpu.SemaphoreType.DMA
    vmem = pltpu.VMEM
    pairs = [dma(s) for s in [(2, chunks), (2, chunks), (pages - 1,), (chunks,), (far,), (chunks,)] for _ in range(2)]
    pairs += [dma, dma]
    pairs += [
        dma(s)
        for s in [(far,), (far,), (2,), (2,), (others,), (2, chunks), (2, chunks), (others, chunks), (others,)]
        for _ in range(2)
    ]
    return pl.pallas_call(
        functools.partial(layer_kernel, sizes),
        out_shape=(
            sds((tokens, share), BF),
            sds((requests, draft, 2 * share), BF),
        ),
        in_specs=[vm, vm, vm, vm, vm, sm, sm, sm, hbm, hbm, hbm, hbm],
        out_specs=(vm,) * 2,
        scratch_shapes=[
            vmem(w_qkv.shape, BF),
            vmem(w_up.shape, BF),
            vmem(w_down.shape, BF),
            vmem(pool.shape, BF),
            dma((5,)),
            vmem((requests, draft, full), BF),
            vmem((requests, draft, share), BF),
            vmem((requests, draft, share), BF),
            vmem((requests, draft, share), BF),
            vmem((requests, draft, draft), F32),
            vmem((requests * draft // 256, draft, 256), BF),
            vmem((1, 128), jnp.int32),
            vmem((pages - 1, 1, 128), jnp.int32),
            pltpu.SMEM((pages - 1, 1, 128), jnp.int32),
            vmem((others, tokens, share), BF),
            vmem((2, draft, share), BF),
            vmem((requests, draft, share), BF),
            vmem((far, 2, draft, share), BF),
            vmem((requests, draft, share), BF),
            vmem((requests, 2, 4 * draft), F32),
            vmem((far, 2 * draft, share), BF),
            vmem((far, 8, 4 * draft), F32),
            vmem((requests, draft, share), BF),
            vmem((requests, 2, 4 * draft), F32),
            vmem((far, 2 * draft, share), BF),
            vmem((far, 8, 4 * draft), F32),
            vmem((requests, draft, share), F32),
            vmem((requests, 4 * draft, 128), F32),
            vmem((others,) + w_own.shape, BF),
            vmem((tokens, share), BF),
            vmem((others, tokens, share), BF),
            vmem((rows, full), BF),
            vmem((tokens, share), BF),
            vmem((tokens, full), BF),
            vmem((others, tokens, share), BF),
            vmem((tokens, share), F32),
            vmem((requests, draft, share), BF),
            vmem((8, rows), F32),
            vmem((others, 8, rows), F32),
        ]
        + pairs,
        compiler_params=pltpu.CompilerParams(
            collective_id=0, has_side_effects=True, vmem_limit_bytes=VMEM_BYTES
        ),
        name="layer",
    )(
        hidden,
        w_own,
        gain1.reshape(1, -1),
        gain2.reshape(1, -1),
        parents,
        accept,
        page_table,
        own_len,
        w_qkv,
        w_up,
        w_down,
        pool,
    )


def shards(
    sizes,
    hidden_in,
    w_qkv,
    w_out,
    first_gain,
    w_up,
    w_down,
    second_gain,
    cache_pool,
    page_table,
    cache_len,
    tree_parent,
    accept_node,
):
    layer_out, kept = layer(
        sizes,
        hidden_in,
        w_out,
        first_gain,
        second_gain,
        tree_parent,
        accept_node,
        page_table,
        cache_len,
        jnp.transpose(w_qkv, (1, 0, 2)),
        w_up,
        w_down,
        cache_pool,
    )
    requests, draft = tree_parent.shape
    return layer_out, kept.reshape(requests, draft, 2, -1)


def solution(mesh):
    placed = (
        P("req", "tp"),
        P(None, None, "tp"),
        P("tp", None),
        P(),
        P(None, "tp"),
        P("tp", None),
        P(),
        P("req", None, None, "tp"),
        P("req", None),
        P("req"),
        P("req", None),
        P("req"),
    )
    sizes = (mesh.shape["req"], mesh.shape["tp"], 8, 4)
    return jax.shard_map(
        functools.partial(shards, sizes),
        mesh=mesh,
        in_specs=placed,
        out_specs=(P("req", "tp"), P("req", None, None, "tp")),
        check_vma=False,
    )
```
